128 devices in a mesh: row: 16 (over y, x), col: 8 (over z, core).
Axes of the slice: x: 4, y: 4, z: 4, core: 2. Of those that a mesh axis runs over, the one named last changes fastest.
Arguments:
- front: float32 [8192, 8192], P('row', 'col'), may hold values from -1 to 4, as said below
- mass_diag: float32 [8192], replicated, may hold values from 0.5 to 1
- shift_bounds: int32 [2], replicated, may hold values from 0 to 255
- vectors: float32 [64, 262144], P(None, ('row', 'col')), may hold values from -12 to 12
- basis: float32 [128, 262144], P(None, ('row', 'col')), may hold values from -6 to 6
- element_dofs: int32 [24, 65536], P(None, ('row', 'col')), may hold values from 0 to 2303
- face_dofs: int32 [256, 128], P(('row', 'col')), may hold values from 0 to 2047
- mass_blocks: float32 [24, 24, 65536], P(None, None, ('row', 'col')), may hold values from -37 to 37
Outputs:
- factor: float32 [8192, 8192], P('row', 'col')
- new_block: float32 [64, 262144], P(None, ('row', 'col'))
- projections: float32 [128, 64], replicated
- cholesky_factor: float32 [64, 64], replicated
The draws below stay inside these ranges and needn't reach their ends.
Inputs may be any that keep to these rules, and one draw needn't show every extreme that they name: Symmetric; every leading principal block of the shifted front is positive definite. `element_dofs`: an entry below 2048 names one of the subdomain's own degrees of freedom; 2048 + j names the j-th of the 256 received ones.
All inputs are finite; a program needn't handle non-finite values.
Results may differ from the reference program's by a relative error of at most 0.0001.
Values sent between devices are 32-bit elements; how exact they have to be, the bound alone decides.
A program may use at most 128 MiB of HBM per device.

```python
import math
import jax
import jax.numpy as jnp
from jax import lax

NF = 8192
PB = 512
NPAN = 2
ND = 2048
NE = 512
NFACE = 128
K = 24
NV = 64
NQ = 128
DOFS = 262144
NEALL = 65536
N_ROW = 16
N_COL = 8


def draw_front(key, part):
    loading_key = jax.random.fold_in(key, 301)
    inner_width = NF // 8
    loadings = jnp.clip(jax.random.normal(loading_key, (NF, inner_width), jnp.float32), -6.0, 6.0)
    gram_part = jnp.dot(loadings, loadings.T, precision=lax.Precision.HIGHEST) / inner_width
    symmetric = 0.5 * (gram_part + gram_part.T)
    diag_index = jnp.arange(NF)
    return symmetric.at[diag_index, diag_index].add(1.2)


def shared_lanczos(key):
    basis_key = jax.random.fold_in(key, 401)
    mixing_key = jax.random.fold_in(key, 402)
    noise_key = jax.random.fold_in(key, 403)
    basis = jnp.clip(jax.random.normal(basis_key, (NQ, DOFS), jnp.float32), -6.0, 6.0)
    noise = jnp.clip(jax.random.normal(noise_key, (NV, DOFS), jnp.float32), -6.0, 6.0)
    mixing = jnp.clip(jax.random.normal(mixing_key, (NV, NQ), jnp.float32), -4.0, 4.0) * (1.2 / math.sqrt(NQ))
    combined = jnp.dot(mixing, basis, precision=lax.Precision.HIGHEST) + noise
    return (basis, jnp.clip(combined, -12.0, 12.0))


def draw_vectors(key, part):
    return shared_lanczos(key)[1]


def draw_basis(key, part):
    return shared_lanczos(key)[0]


def draw_mass_blocks(key, part):
    entry_key = jax.random.fold_in(key, 501)
    raw_values = jnp.clip(jax.random.normal(entry_key, (K, K, NEALL), jnp.float32), -6.0, 6.0)
    blocks = jnp.einsum('ace,bce->abe', raw_values, raw_values, precision=lax.Precision.HIGHEST) / K
    return blocks + 0.5 * jnp.eye(K, dtype=jnp.float32)[:, :, None]


def place_ends(result, own_key, least, largest):
    place = [jax.random.randint(jax.random.fold_in(own_key, axis), (), 0, length) for axis, length in enumerate(result.shape)]
    widest = result.shape.index(max(result.shape))
    next_to = place[:widest] + [(place[widest] + 1) % result.shape[widest]] + place[widest + 1:]
    return result.at[tuple(place)].set(least).at[tuple(next_to)].set(largest)


def setup_inputs(seed: int = 0) -> dict:
    arg_keys = jax.random.split(jax.random.key(seed), 9)
    return {
        "front": draw_front(jax.random.fold_in(arg_keys[8], 71), 0),
        "mass_diag": jnp.clip(jax.random.uniform(arg_keys[1], (NF,), jnp.float32, 0.5, 1.0), 0.5, 1.0),
        "shift_bounds": jax.random.randint(arg_keys[2], (2,), 0, 256).astype(jnp.int32),
        "vectors": draw_vectors(jax.random.fold_in(arg_keys[8], 71), 0),
        "basis": draw_basis(jax.random.fold_in(arg_keys[8], 71), 0),
        "element_dofs": place_ends(jax.random.randint(arg_keys[5], (K, NEALL), 0, ND + 2 * (ND // 16)), jax.random.fold_in(arg_keys[5], 1), 0, (ND + 2 * (ND // 16)) - 1).astype(jnp.int32),
        "face_dofs": place_ends(jax.random.randint(arg_keys[6], (2 * N_ROW * N_COL, NFACE), 0, ND), jax.random.fold_in(arg_keys[6], 1), 0, ND - 1).astype(jnp.int32),
        "mass_blocks": draw_mass_blocks(jax.random.fold_in(arg_keys[8], 71), 0),
    }


PRECISE = lax.Precision.HIGHEST

def product(left, right):
    return jnp.dot(left.astype(jnp.float32), right.astype(jnp.float32), precision=PRECISE, preferred_element_type=jnp.float32)

def invert_block(block):
    factor = jnp.linalg.cholesky(block)
    identity = jnp.eye(block.shape[0], dtype=block.dtype)
    return jax.scipy.linalg.cho_solve((factor, True), identity)

def factor_front(front, mass_diag, shift_bounds):
    front_order = front.shape[0]
    shift_value = (shift_bounds[0] + shift_bounds[1]).astype(front.dtype) / 510.0
    diag_index = jnp.arange(front_order)
    matrix = front.at[diag_index, diag_index].add(-(shift_value * mass_diag))
    for panel_index in range(NPAN):
        begin_at = panel_index * PB
        end_at = begin_at + PB
        inverse = invert_block(matrix[begin_at:end_at, begin_at:end_at])
        left_factor = product(matrix[end_at:, begin_at:end_at], inverse)
        right_factor = product(inverse, matrix[begin_at:end_at, end_at:])
        trailing = matrix[end_at:, end_at:] - product(left_factor, matrix[begin_at:end_at, end_at:])
        matrix = matrix.at[end_at:, end_at:].set(trailing)
        matrix = matrix.at[end_at:, begin_at:end_at].set(left_factor)
        matrix = matrix.at[begin_at:end_at, end_at:].set(right_factor)
    return matrix

def pick_faces(subdomain, face_list):
    return subdomain[:, face_list]

def mass_apply(vectors, element_dofs, face_dofs, mass_blocks):
    groups = N_ROW * N_COL
    owned = vectors.shape[1] // groups
    by_group = vectors.reshape(NV, groups, owned).transpose(1, 0, 2)
    face_lists = face_dofs.reshape(groups, 2, NFACE)
    outgoing = jax.vmap(pick_faces)(by_group, face_lists)
    empty = jnp.zeros((1, NV, NFACE), vectors.dtype)
    from_before = jnp.concatenate([empty, outgoing[:-1, :, 1]], axis=0)
    from_after = jnp.concatenate([outgoing[1:, :, 0], empty], axis=0)
    extended = jnp.concatenate([by_group, from_before, from_after], axis=2)
    element_map = element_dofs.reshape(K, groups, NE).transpose(1, 0, 2)
    local_mass = mass_blocks.reshape(K, K, groups, NE).transpose(2, 0, 1, 3)

    def apply_one(pieces):
        ext_part, dof_map, mass_part = pieces
        gathered = ext_part[:, dof_map]
        contrib = jnp.einsum('abe,vbe->vae', mass_part, gathered, precision=PRECISE)
        summed = jnp.zeros_like(ext_part).at[:, dof_map].add(contrib)
        return summed[:, :owned]
    applied = lax.map(apply_one, (extended, element_map, local_mass))
    return applied.transpose(1, 0, 2).reshape(NV, groups * owned)

def reference(front, mass_diag, shift_bounds, vectors, basis, element_dofs, face_dofs, mass_blocks):
    factor = factor_front(front, mass_diag, shift_bounds)
    applied = mass_apply(vectors, element_dofs, face_dofs, mass_blocks)
    projections = product(basis, applied.T) / DOFS
    corrected = applied - product(projections.T, basis)
    gram_matrix = product(corrected, corrected.T) / DOFS
    cholesky_factor = jnp.linalg.cholesky(gram_matrix)
    new_block = jax.scipy.linalg.solve_triangular(cholesky_factor, corrected, lower=True)
    return (factor, new_block, projections, cholesky_factor)
```

```python
import functools

import jax
import jax.numpy as jnp
from jax import lax
from jax.experimental import pallas as pl
from jax.experimental.pallas import tpu as pltpu
from jax.sharding import PartitionSpec as P

MESH = pl.DeviceIdType.MESH
HI = lax.Precision.HIGHEST
F32 = jnp.float32
BF16 = jnp.bfloat16
PB = 512
TOTAL = 262144.0
VM = pl.BlockSpec(memory_space=pltpu.VMEM)
ANY = pl.BlockSpec(memory_space=pl.ANY)
NT = (((1,), (1,)), ((), ()))
NN = (((1,), (0,)), ((), ()))
TN = (((0,), (0,)), ((), ()))


def dot(a, b, dims=NN):
    return lax.dot_general(a, b, dims, precision=HI, preferred_element_type=F32)


def split(a):
    high = a.astype(BF16)
    return high, (a - high.astype(F32)).astype(BF16)


def dot3(a, b, dims=NN):
    (ah, al), (bh, bl) = a, b

    def one(l, r):
        return lax.dot_general(l, r, dims, preferred_element_type=F32)

    return one(ah, bh) + (one(ah, bl) + one(al, bh))


def place():
    row, col = lax.axis_index("row"), lax.axis_index("col")
    return row % 4, row // 4, col // 2, col % 2


def device(x, y, z, k):
    return ((y % 4) * 4 + (x % 4), (z % 4) * 2 + k)


def enter(peers):
    barrier = pltpu.get_barrier_semaphore()
    for peer in peers:
        pl.semaphore_signal(barrier, inc=1, device_id=peer, device_id_type=MESH)
    return barrier


def remote(src, dst, send, recv, peer):
    return pltpu.make_async_remote_copy(
        src_ref=src, dst_ref=dst, send_sem=send, recv_sem=recv, device_id=peer, device_id_type=MESH
    )


def pick(ext_ref, index, chunks):
    low = jnp.broadcast_to(index & 127, (64, 128))
    high = jnp.broadcast_to(index >> 7, (64, 128))
    found = jnp.take_along_axis(ext_ref[:, 0:128], low, axis=1)
    for c in range(1, chunks):
        found = jnp.where(high == c, jnp.take_along_axis(ext_ref[:, 128 * c : 128 * c + 128], low, axis=1), found)
    return found


def travel_kernel(
    front, vectors, dofs, faces, mass,
    xr, rp, pv, applied,
    ext, fs, got, wide, hot,
    rp_in, pv_in, xr_in, rpx, rpy, pvz, pvc, xrz, xrc, face_out, face_in,
):
    x, y, z, k = place()
    me = lax.axis_index("row") * 8 + lax.axis_index("col")
    before, after = (me + 127) % 128, (me + 1) % 128
    peers = [
        device(x + 1, y, z, k), device(x + 3, y, z, k), device(x, y + 1, z, k), device(x, y + 3, z, k),
        device(x, y, z + 1, k), device(x, y, z + 3, k), device(x, y, z, 1 - k),
        (before // 8, before % 8), (after // 8, after % 8),
    ]
    barrier = enter(peers)

    def rows(ref, m):
        return ref.at[pl.ds(pl.multiple_of(m * 64, 64), 64), :]

    def half(ref, m):
        return ref.at[pl.ds(pl.multiple_of(m * 64, 64), 64), pl.ds(512, 512)]

    for source in range(2):
        @pl.when((x == source) & (y == 0))
        def _():
            for m in range(8):
                pltpu.make_async_copy(rows(front, m), rows(rp, m + 8 * source), rp_in.at[m + 8 * source]).start()

    @pl.when((z == 0) & (k == 0))
    def _():
        for m in range(8):
            pltpu.make_async_copy(rows(front, m), rows(xr, m), xr_in.at[m]).start()

    ext[:, 0:2048] = vectors[...]
    fs[0] = pick(ext, faces[0], 16)
    fs[1] = pick(ext, faces[1], 16)

    @pl.when(me == 0)
    def _():
        ext[:, 2048:2176] = jnp.zeros((64, 128), F32)

    @pl.when(me == 127)
    def _():
        ext[:, 2176:2304] = jnp.zeros((64, 128), F32)

    pl.semaphore_wait(barrier, len(peers))

    to_before = remote(fs.at[0], ext.at[:, pl.ds(2176, 128)], face_out.at[0], face_in.at[0], (before // 8, before % 8))
    to_after = remote(fs.at[1], ext.at[:, pl.ds(2048, 128)], face_out.at[1], face_in.at[1], (after // 8, after % 8))

    @pl.when(me > 0)
    def _():
        to_before.start()

    @pl.when(me < 127)
    def _():
        to_after.start()

    def rp_hop(m):
        d = 1 - 2 * (m % 2)
        hx = ((x - m // 8) * d + 8) % 4
        hy = (y * d + 8) % 4
        c = rows(rp, m)
        along_x = remote(c, c, rpx.at[m], rp_in.at[m], device(x + d + 4, y, z, k))
        along_y = remote(c, c, rpy.at[m], rp_in.at[m], device(x, y + d + 4, z, k))
        return along_x, (y == 0) & (hx < 3), along_y, hy < 3

    def rp_event(m):
        ax, px, ay, py = rp_hop(m)
        ax.wait_recv()

        @pl.when(px)
        def _():
            ax.start()

        @pl.when(py)
        def _():
            ay.start()

    origin = (z == 0) & (k == 0)

    def pv_copies(m, view, src):
        d = 1 - 2 * (m % 2)
        along_z = remote(view(src, m), view(pv, m), pvz.at[m], pv_in.at[m], device(x, y, z + d + 4, k))
        across = remote(view(src, m), view(pv, m), pvc.at[m], pv_in.at[m], device(x, y, z, 1 - k))
        return along_z, (k == 0) & ((z * d + 8) % 4 < 3), across, k == 0

    def pv_case(m, act):
        @pl.when((m < 8) & origin)
        def _():
            act(pv_copies(m, rows, rp), True)

        @pl.when((m < 8) & ~origin)
        def _():
            act(pv_copies(m, rows, pv), False)

        @pl.when((m >= 8) & origin)
        def _():
            act(pv_copies(m, half, rp), True)

        @pl.when((m >= 8) & ~origin)
        def _():
            act(pv_copies(m, half, pv), False)

    def pv_event(m):
        def act(copies, first):
            az, pz, ac, pc = copies
            if not first:
                az.wait_recv()

            @pl.when(pz)
            def _():
                az.start()

            @pl.when(pc)
            def _():
                ac.start()

        pv_case(m, act)

    def xr_hop(m):
        d = 1 - 2 * (m % 2)
        c = rows(xr, m)
        along_z = remote(c, c, xrz.at[m], xr_in.at[m], device(x, y, z + d + 4, k))
        across = remote(c, c, xrc.at[m], xr_in.at[m], device(x, y, z, 1 - k))
        return along_z, (k == 0) & ((z * d + 8) % 4 < 3), across, k == 0

    def xr_event(m):
        az, pz, ac, pc = xr_hop(m)
        az.wait_recv()

        @pl.when(pz)
        def _():
            az.start()

        @pl.when(pc)
        def _():
            ac.start()

    def order(j):
        return 2 * (j // 4) + j % 2 + 8 * ((j % 4) // 2)

    def hook(h):
        j = h // 4

        @pl.when((h % 4 == 0) & (j < 16))
        def _():
            rp_event(order(j))

        @pl.when((h % 4 == 1) & (j >= 2) & (j < 18))
        def _():
            pv_event(order(j - 2))

        @pl.when((h % 4 == 2) & (j >= 10) & (j < 18))
        def _():
            xr_event(j - 10)

    @pl.when(me > 0)
    def _():
        to_before.wait_send()
        to_after.wait_recv()

    @pl.when(me < 127)
    def _():
        to_after.wait_send()
        to_before.wait_recv()

    applied[...] = jnp.zeros_like(applied)
    sub = lax.broadcasted_iota(jnp.int32, (256, 128), 0)

    def chunk(e, _):
        es = pl.ds(pl.multiple_of(e * 128, 128), 128)

        def gather(b, _):
            hook(e * 24 + b)
            got[b] = pick(ext, dofs[b, :, es], 18)
            return 0

        lax.fori_loop(0, 24, gather, 0)

        def contract(a4, _):
            total = [jnp.zeros((64, 128), F32) for _ in range(4)]
            for b in range(24):
                g = got[b]
                for q in range(4):
                    total[q] = total[q] + mass[a4 * 4 + q, pl.ds(b, 1), es] * g
            for q in range(4):
                a = a4 * 4 + q
                index = dofs[a, :, es]
                high = jnp.broadcast_to(index >> 8, (64, 128))
                low = jnp.broadcast_to(index & 255, (256, 128))
                big = total[q].astype(BF16).astype(F32)
                small = total[q] - big
                ps = pl.ds(pl.multiple_of(a * 128, 128), 128)
                for c in range(8):
                    here = high == c
                    wide[64 * c : 64 * c + 64, ps] = jnp.where(here, big, 0.0).astype(BF16)
                    wide[512 + 64 * c : 576 + 64 * c, ps] = jnp.where(here, small, 0.0).astype(BF16)
                hot[:, ps] = jnp.where(sub == low, 1.0, 0.0).astype(BF16)
            return 0

        lax.fori_loop(0, 6, contract, 0)
        out = lax.dot_general(wide[...], hot[...], NT, preferred_element_type=F32)
        for c in range(8):
            applied[:, 256 * c : 256 * c + 256] += out[64 * c : 64 * c + 64] + out[512 + 64 * c : 576 + 64 * c]
        return 0

    lax.fori_loop(0, 4, chunk, 0)

    def drain(m, _):
        ax, px, ay, py = rp_hop(m)

        @pl.when(px)
        def _():
            ax.wait_send()

        @pl.when(py)
        def _():
            ay.wait_send()

        def act(copies, first):
            az, pz, ac, pc = copies

            @pl.when(pz)
            def _():
                az.wait_send()

            @pl.when(pc)
            def _():
                ac.wait_send()

        pv_case(m, act)
        return 0

    lax.fori_loop(0, 16, drain, 0)

    def drain_x(m, _):
        az, pz, ac, pc = xr_hop(m)

        @pl.when(pz)
        def _():
            az.wait_send()

        @pl.when(pc)
        def _():
            ac.wait_send()
        return 0

    lax.fori_loop(0, 8, drain_x, 0)


def travel(front, vectors, dofs, faces, mass):
    dma = pltpu.SemaphoreType.DMA
    return pl.pallas_call(
        travel_kernel,
        out_shape=(
            jax.ShapeDtypeStruct((512, 1024), F32),
            jax.ShapeDtypeStruct((1024, 1024), F32),
            jax.ShapeDtypeStruct((1024, 1024), F32),
            jax.ShapeDtypeStruct((64, 2048), F32),
        ),
        in_specs=[VM] * 5,
        out_specs=(ANY, ANY, ANY, VM),
        scratch_shapes=[
            pltpu.VMEM((64, 2304), F32),
            pltpu.VMEM((2, 64, 128), F32),
            pltpu.VMEM((24, 64, 128), F32),
            pltpu.VMEM((1024, 3072), BF16),
            pltpu.VMEM((256, 3072), BF16),
            dma((16,)), dma((16,)), dma((8,)),
            dma((16,)), dma((16,)), dma((16,)), dma((16,)), dma((8,)), dma((8,)),
            dma((2,)), dma((2,)),
        ],
        compiler_params=pltpu.CompilerParams(collective_id=1, has_side_effects=True, vmem_limit_bytes=50 << 20),
    )(front, vectors, dofs, faces, mass)


def lanes(v, j):
    return jnp.broadcast_to(v[:, j : j + 1], (8, 128))


def subs(v, j):
    return jnp.broadcast_to(v[j : j + 1, :], (8, 128))


def tree(t):
    while len(t) > 1:
        t = [t[i] + t[i + 1] for i in range(0, len(t), 2)]
    return t[0]


def inverse8(cols, row8):
    cols = list(cols)
    for j in range(8):
        ip = 1.0 / subs(cols[j], j)
        pivot = cols[j]
        for m in range(8):
            if m != j:
                r = subs(cols[m], j) * ip
                cols[m] = jnp.where(row8 == j, r, cols[m] - pivot * r)
        cols[j] = jnp.where(row8 == j, ip, -pivot * ip)
    return cols


def inverse128(block):
    lane8 = lax.broadcasted_iota(jnp.int32, (8, 128), 1)
    row8 = lax.broadcasted_iota(jnp.int32, (8, 128), 0)
    v = [block[8 * i : 8 * i + 8] for i in range(16)]
    for kb in range(16):
        k0 = 8 * kb
        w = v[kb]
        cols = inverse8([lanes(w, k0 + j) for j in range(8)], row8)
        r = tree([cols[m] * subs(w, m) for m in range(8)])
        for m in range(8):
            r = jnp.where(lane8 == k0 + m, cols[m], r)
        rs = [subs(r, m) for m in range(8)]
        own = (lane8 // 8) == kb
        for i in list(range(kb + 1, 16)) + list(range(kb)):
            o = v[i]
            v[i] = jnp.where(own, 0.0, o) - tree([lanes(o, k0 + m) * rs[m] for m in range(8)])
        v[kb] = r
    return jnp.concatenate(v, 0)


def invert_in_place(ref):
    def body(b, _):
        s = pl.ds(pl.multiple_of(b * 128, 128), 128)
        d = inverse128(ref[s, s])
        c = ref[:, s]
        r = dot(d, ref[s, :])
        ref[...] = ref[...] - dot(c, r)
        ref[s, :] = r
        ref[:, s] = -dot(c, d)
        ref[s, s] = d
        return 0

    lax.fori_loop(0, 4, body, 0)


def update_kernel(bounds, diag, front, xr, rp, pv, out, a11, a12, a22, sem):
    row, col = lax.axis_index("row"), lax.axis_index("col")
    shift = (bounds[0] + bounds[1]).astype(F32) / 510.0

    def fetch(src):
        copies = [
            pltpu.make_async_copy(src.at[pl.ds(0, 512), pl.ds(0, 512)], a11, sem.at[0]),
            pltpu.make_async_copy(src.at[pl.ds(0, 512), pl.ds(512, 512)], a12, sem.at[1]),
            pltpu.make_async_copy(src.at[pl.ds(512, 512), pl.ds(512, 512)], a22, sem.at[2]),
        ]
        for c in copies:
            c.start()
        for c in copies:
            c.wait()

    @pl.when(col == 0)
    def _():
        fetch(rp)

    @pl.when(col > 0)
    def _():
        fetch(pv)

    ri = lax.broadcasted_iota(jnp.int32, (512, 512), 0)
    ci = lax.broadcasted_iota(jnp.int32, (512, 512), 1)
    a11[...] = a11[...] - jnp.where(ri == ci, shift * diag[:, 0:512], 0.0)
    a22[...] = a22[...] - jnp.where(ri == ci, shift * diag[:, 512:1024], 0.0)

    @pl.when((row == 0) & (col == 0))
    def _():
        out[:, 0:512] = a11[...]

    invert_in_place(a11)
    w = dot(a11[...], a12[...])
    s22 = a22[...] - dot(a12[...], w, TN)
    a12[...] = w
    a22[...] = s22

    @pl.when((row == 1) & (col == 0))
    def _():
        out[:, 0:512] = jnp.transpose(w)
        out[:, 512:1024] = s22

    @pl.when((row == 0) & (col == 0))
    def _():
        out[:, 512:1024] = w

    invert_in_place(a22)

    @pl.when(row >= 2)
    def _():
        x1, x2 = split(xr[:, 0:512]), xr[:, 512:1024]
        i2, ws = split(a22[...]), split(a12[...])
        l1 = dot3(x1, split(a11[...]))
        l2 = dot3(split(x2 - dot3(x1, ws)), i2)

        @pl.when(col == 0)
        def _():
            out[:, 0:512] = l1
            out[:, 512:1024] = l2

        @pl.when(col > 0)
        def _():
            l2s = split(l2)
            t1 = split(l1 - dot3(l2s, ws, NT))
            j = lax.broadcasted_iota(jnp.int32, (512, 1024), 1)
            i = lax.broadcasted_iota(jnp.int32, (512, 1024), 0)
            mine = diag[:, pl.ds(pl.multiple_of(col * 1024, 1024), 1024)]
            tile = front[...] - jnp.where(j + col * 1024 == i + row * 512, shift * mine, 0.0)
            out[...] = tile - dot3(t1, split(rp[0:512, :])) - dot3(l2s, split(rp[512:1024, :]))

    @pl.when((row == 0) & (col > 0))
    def _():
        out[...] = dot3(split(a11[...]), split(rp[0:512, :]))

    @pl.when((row == 1) & (col > 0))
    def _():
        out[...] = dot3(split(a22[...]), split(rp[512:1024, :] - dot3(split(a12[...]), split(rp[0:512, :]), TN)))


def update(bounds, diag, front, xr, rp, pv):
    return pl.pallas_call(
        update_kernel,
        out_shape=jax.ShapeDtypeStruct((512, 1024), F32),
        in_specs=[pl.BlockSpec(memory_space=pltpu.SMEM), VM, VM, VM, VM, ANY],
        out_specs=VM,
        scratch_shapes=[pltpu.VMEM((512, 512), F32)] * 3 + [pltpu.SemaphoreType.DMA((3,))],
        compiler_params=pltpu.CompilerParams(vmem_limit_bytes=56 << 20),
    )(bounds, diag, front, xr, rp, pv)


def lanczos_kernel(applied, basis, new, proj, chol, acc, slots, core_slot, send, recv):
    x, y, z, k = place()
    peers = [device(x + s, y, z, k) for s in (1, 2, 3)]
    peers += [device(x, y + s, z, k) for s in (1, 2, 3)]
    peers += [device(x, y, z + s, k) for s in (1, 2, 3)]
    peers += [device(x, y, z, 1 - k)]
    barrier = enter(peers)
    pl.semaphore_wait(barrier, len(peers))

    def reduce(phase, value):
        acc[phase, 0] = value
        c = remote(acc.at[phase, 0], core_slot.at[phase], send.at[phase, 9], recv.at[phase, 9], peers[9])
        c.start()
        c.wait()
        value = value + core_slot[phase]
        for axis, coordinate in enumerate((x, y, z)):
            acc[phase, axis + 1] = value
            copies = []
            for s in (1, 2, 3):
                n = 3 * axis + s - 1
                copies.append(
                    remote(
                        acc.at[phase, axis + 1], slots.at[phase, n], send.at[phase, n], recv.at[phase, n], peers[n]
                    )
                )
            for c in copies:
                c.start()
            for c in copies:
                c.wait()
            parts = [value] + [slots[phase, 3 * axis + s - 1] for s in (1, 2, 3)]
            ordered = []
            for q in range(4):
                away = (coordinate - q + 4) % 4
                part = parts[3]
                for s in (2, 1, 0):
                    part = jnp.where(away == s, parts[s], part)
                ordered.append(part)
            value = (ordered[0] + ordered[1]) + (ordered[2] + ordered[3])
        return value

    a = applied[...]
    pt = reduce(0, dot(a, basis[...], NT)) / TOTAL
    proj[...] = jnp.transpose(pt)
    corrected = a - dot(pt, basis[...])
    new[...] = corrected
    gram = dot(corrected, corrected, NT)
    gram = reduce(1, jnp.concatenate([gram, jnp.zeros((64, 64), F32)], axis=1)) / TOTAL

    lane8 = lax.broadcasted_iota(jnp.int32, (8, 128), 1)
    row8 = lax.broadcasted_iota(jnp.int32, (8, 128), 0)
    v = [gram[8 * i : 8 * i + 8] + jnp.where(lane8 == row8 + 64 + 8 * i, 1.0, 0.0) for i in range(8)]
    for kb in range(8):
        k0 = 8 * kb
        w = v[kb]
        first = [lanes(w, k0 + j) for j in range(8)]
        cols = inverse8(first, row8)
        r = tree([cols[m] * subs(w, m) for m in range(8)])
        rs = [subs(r, m) for m in range(8)]
        for i in range(kb + 1, 8):
            o = v[i]
            v[i] = o - tree([lanes(o, k0 + m) * rs[m] for m in range(8)])
        c = list(first)
        scale = jnp.zeros((8, 128), F32)
        for j in range(8):
            p = subs(c[j], j)
            f = jnp.where(row8 > j, c[j] / p, 0.0)
            w = w - f * subs(w, j)
            for m in range(j + 1, 8):
                c[m] = c[m] - f * subs(c[m], j)
            scale = jnp.where(row8 == j, p, scale)
        v[kb] = w / jnp.sqrt(scale)
    full = jnp.concatenate(v, 0)
    upper, inverse = full[:, 0:64], full[:, 64:128]
    ri = lax.broadcasted_iota(jnp.int32, (64, 64), 0)
    ci = lax.broadcasted_iota(jnp.int32, (64, 64), 1)
    chol[...] = jnp.transpose(jnp.where(ri <= ci, upper, 0.0))
    new[...] = dot(inverse, new[...])


def lanczos(applied, basis):
    dma = pltpu.SemaphoreType.DMA
    return pl.pallas_call(
        lanczos_kernel,
        out_shape=(
            jax.ShapeDtypeStruct((64, 2048), F32),
            jax.ShapeDtypeStruct((128, 64), F32),
            jax.ShapeDtypeStruct((64, 64), F32),
        ),
        in_specs=[VM, VM],
        out_specs=(VM, VM, VM),
        scratch_shapes=[
            pltpu.VMEM((2, 4, 64, 128), F32),
            pltpu.VMEM((2, 9, 64, 128), F32),
            pltpu.VMEM((2, 64, 128), F32),
            dma((2, 10)), dma((2, 10)),
        ],
        compiler_params=pltpu.CompilerParams(collective_id=2, has_side_effects=True, vmem_limit_bytes=40 << 20),
    )(applied, basis)


def shards(front, mass_diag, shift_bounds, vectors, basis, element_dofs, face_dofs, mass_blocks):
    xr, rp, pv, applied = travel(
        front, vectors, element_dofs.reshape(24, 1, 512), face_dofs.reshape(2, 1, 128), mass_blocks
    )
    new_block, projections, cholesky_factor = lanczos(applied, basis)
    factor = update(shift_bounds, mass_diag.reshape(1, -1), front, xr, rp, pv)
    return factor, new_block, projections, cholesky_factor


def solution(mesh):
    placed = (
        P("row", "col"),
        P(),
        P(),
        P(None, ("row", "col")),
        P(None, ("row", "col")),
        P(None, ("row", "col")),
        P(("row", "col"), None),
        P(None, None, ("row", "col")),
    )
    return jax.shard_map(
        shards,
        mesh=mesh,
        in_specs=placed,
        out_specs=(P("row", "col"), P(None, ("row", "col")), P(), P()),
        check_vma=False,
    )
```

```python
import functools

import jax
import jax.numpy as jnp
from jax import lax
from jax.experimental import pallas as pl
from jax.experimental.pallas import tpu as pltpu
from jax.sharding import PartitionSpec as P

MESH = pl.DeviceIdType.MESH
HI = lax.Precision.HIGHEST
F32 = jnp.float32
BF16 = jnp.bfloat16
STEP = 16
LAG = 2
NSTEP = 256 // STEP
TOTAL = 262144.0
VM = pl.BlockSpec(memory_space=pltpu.VMEM)
ANY = pl.BlockSpec(memory_space=pl.ANY)
NT = (((1,), (1,)), ((), ()))
NN = (((1,), (0,)), ((), ()))
TN = (((0,), (0,)), ((), ()))


def dot(a, b, dims=NN):
    return lax.dot_general(a, b, dims, precision=HI, preferred_element_type=F32)


def split(a):
    high = a.astype(BF16)
    return high, (a - high.astype(F32)).astype(BF16)


def dot3(a, b, dims=NN):
    (ah, al), (bh, bl) = a, b

    def one(l, r):
        return lax.dot_general(l, r, dims, preferred_element_type=F32)

    return one(ah, bh) + (one(ah, bl) + one(al, bh))


def place():
    row, col = lax.axis_index("row"), lax.axis_index("col")
    return row % 4, row // 4, col // 2, col % 2


def device(x, y, z, k):
    return ((y % 4) * 4 + (x % 4), (z % 4) * 2 + k)


def enter(peers):
    barrier = pltpu.get_barrier_semaphore()
    for peer in peers:
        pl.semaphore_signal(barrier, inc=1, device_id=peer, device_id_type=MESH)
    return barrier


def remote(src, dst, send, recv, peer):
    return pltpu.make_async_remote_copy(
        src_ref=src, dst_ref=dst, send_sem=send, recv_sem=recv, device_id=peer, device_id_type=MESH
    )


def pick(ext_ref, index, chunks):
    low = jnp.broadcast_to(index & 127, (64, 128))
    high = jnp.broadcast_to(index >> 7, (64, 128))
    found = jnp.take_along_axis(ext_ref[:, 0:128], low, axis=1)
    for c in range(1, chunks):
        found = jnp.where(high == c, jnp.take_along_axis(ext_ref[:, 128 * c : 128 * c + 128], low, axis=1), found)
    return found


def travel_kernel(
    front, vectors, dofs, faces, mass,
    xr, rp, pv, applied,
    ext, fs, got, wide, hot,
    rp_in, pv_in, xr_in, rpx, rpy, pvz, pvc, xrz, xrc, face_out, face_in,
):
    x, y, z, k = place()
    me = lax.axis_index("row") * 8 + lax.axis_index("col")
    before, after = (me + 127) % 128, (me + 1) % 128
    peers = [
        device(x + 1, y, z, k), device(x + 3, y, z, k), device(x, y + 1, z, k), device(x, y + 3, z, k),
        device(x, y, z + 1, k), device(x, y, z + 3, k), device(x, y, z, 1 - k),
        (before // 8, before % 8), (after // 8, after % 8),
    ]
    barrier = enter(peers)

    def rows(ref, first, count=STEP):
        return ref.at[pl.ds(pl.multiple_of(first, STEP), count), :]

    def half(ref, first, count=STEP):
        return ref.at[pl.ds(pl.multiple_of(first, STEP), count), pl.ds(512, 512)]

    def ways():
        return ((0, 1), (1, -1))

    for source in range(2):
        @pl.when((x == source) & (y == 0))
        def _():
            for w, _ in ways():
                for i in range(NSTEP):
                    own = 256 * w + STEP * i
                    pltpu.make_async_copy(
                        rows(front, own), rows(rp, 512 * source + own), rp_in.at[2 * source + w, i]
                    ).start()

    @pl.when((z == 0) & (k == 0))
    def _():
        for w, _ in ways():
            for i in range(NSTEP):
                own = 256 * w + STEP * i
                pltpu.make_async_copy(rows(front, own), rows(xr, own), xr_in.at[w, i]).start()

    ext[:, 0:2048] = vectors[...]
    fs[0] = pick(ext, faces[0], 16)
    fs[1] = pick(ext, faces[1], 16)

    @pl.when(me == 0)
    def _():
        ext[:, 2048:2176] = jnp.zeros((64, 128), F32)

    @pl.when(me == 127)
    def _():
        ext[:, 2176:2304] = jnp.zeros((64, 128), F32)

    pl.semaphore_wait(barrier, len(peers))

    to_before = remote(fs.at[0], ext.at[:, pl.ds(2176, 128)], face_out.at[0], face_in.at[0], (before // 8, before % 8))
    to_after = remote(fs.at[1], ext.at[:, pl.ds(2048, 128)], face_out.at[1], face_in.at[1], (after // 8, after % 8))

    @pl.when(me > 0)
    def _():
        to_before.start()

    @pl.when(me < 127)
    def _():
        to_after.start()

    origin = (z == 0) & (k == 0)

    def rp_hop(source, w, d, i, count=STEP):
        n = 2 * source + w
        c = rows(rp, 512 * source + 256 * w + STEP * i, count)
        hx, hy = ((x - source) * d + 8) % 4, (y * d + 8) % 4
        return (
            LAG * (hx + hy),
            remote(c, c, rpx.at[n], rp_in.at[n, i], device(x + d + 4, y, z, k)), (y == 0) & (hx < 3),
            remote(c, c, rpy.at[n], rp_in.at[n, i], device(x, y + d + 4, z, k)), hy < 3,
        )

    def pv_hop(source, w, d, i, src, count=STEP):
        n = 2 * source + w
        view = half if source else rows
        first = 512 * source + 256 * w + STEP * i
        hz = (z * d + 8) % 4
        return (
            LAG * (hz + k),
            remote(view(src, first, count), view(pv, first, count), pvz.at[n], pv_in.at[n, i], device(x, y, z + d + 4, k)),
            (k == 0) & (hz < 3),
            remote(view(src, first, count), view(pv, first, count), pvc.at[n], pv_in.at[n, i], device(x, y, z, 1 - k)),
            k == 0,
        )

    def xr_hop(w, d, i, count=STEP):
        c = rows(xr, 256 * w + STEP * i, count)
        hz = (z * d + 8) % 4
        return (
            LAG * (hz + k),
            remote(c, c, xrz.at[w], xr_in.at[w, i], device(x, y, z + d + 4, k)), (k == 0) & (hz < 3),
            remote(c, c, xrc.at[w], xr_in.at[w, i], device(x, y, z, 1 - k)), k == 0,
        )

    def pass_on(hop, received=True):
        _, one, p1, two, p2 = hop
        if received:
            one.wait_recv()

        @pl.when(p1)
        def _():
            one.start()

        @pl.when(p2)
        def _():
            two.start()

    def slot(t):
        for w, d in ways():
            i = t - xr_hop(w, d, 0)[0]

            @pl.when((i >= 0) & (i < NSTEP))
            def _():
                pass_on(xr_hop(w, d, i))

        for source in range(2):
            for w, d in ways():
                i = t - rp_hop(source, w, d, 0)[0]

                @pl.when((i >= 0) & (i < NSTEP))
                def _():
                    pass_on(rp_hop(source, w, d, i))

        for source in range(2):
            for w, d in ways():
                i = t - rp_hop(source, w, d, 0)[0] - pv_hop(source, w, d, 0, pv)[0]
                due = (i >= 0) & (i < NSTEP)

                @pl.when(due & origin)
                def _():
                    pass_on(pv_hop(source, w, d, i, rp), False)

                @pl.when(due & ~origin)
                def _():
                    pass_on(pv_hop(source, w, d, i, pv))

    def hook(h):
        @pl.when((h % 2 == 0) & (h < 2 * (NSTEP + 10 * LAG)))
        def _():
            slot(h // 2)

    @pl.when(me > 0)
    def _():
        to_before.wait_send()
        to_after.wait_recv()

    @pl.when(me < 127)
    def _():
        to_after.wait_send()
        to_before.wait_recv()

    applied[...] = jnp.zeros_like(applied)
    sub = lax.broadcasted_iota(jnp.int32, (256, 128), 0)

    def chunk(e, _):
        es = pl.ds(pl.multiple_of(e * 128, 128), 128)

        def gather(b, _):
            hook(e * 24 + b)
            got[b] = pick(ext, dofs[b, :, es], 18)
            return 0

        lax.fori_loop(0, 24, gather, 0)

        def contract(a4, _):
            total = [jnp.zeros((64, 128), F32) for _ in range(4)]
            for b in range(24):
                g = got[b]
                for q in range(4):
                    total[q] = total[q] + mass[a4 * 4 + q, pl.ds(b, 1), es] * g
            for q in range(4):
                a = a4 * 4 + q
                index = dofs[a, :, es]
                high = jnp.broadcast_to(index >> 8, (64, 128))
                low = jnp.broadcast_to(index & 255, (256, 128))
                big = total[q].astype(BF16).astype(F32)
                small = total[q] - big
                ps = pl.ds(pl.multiple_of(a * 128, 128), 128)
                for c in range(8):
                    here = high == c
                    wide[64 * c : 64 * c + 64, ps] = jnp.where(here, big, 0.0).astype(BF16)
                    wide[512 + 64 * c : 576 + 64 * c, ps] = jnp.where(here, small, 0.0).astype(BF16)
                hot[:, ps] = jnp.where(sub == low, 1.0, 0.0).astype(BF16)
            return 0

        lax.fori_loop(0, 6, contract, 0)
        out = lax.dot_general(wide[...], hot[...], NT, preferred_element_type=F32)
        for c in range(8):
            applied[:, 256 * c : 256 * c + 256] += out[64 * c : 64 * c + 64] + out[512 + 64 * c : 576 + 64 * c]
        return 0

    lax.fori_loop(0, 4, chunk, 0)

    def drain(hop):
        _, one, p1, two, p2 = hop

        @pl.when(p1)
        def _():
            one.wait_send()

        @pl.when(p2)
        def _():
            two.wait_send()

    for w, d in ways():
        drain(xr_hop(w, d, 0, 256))
        for source in range(2):
            drain(rp_hop(source, w, d, 0, 256))
            drain(pv_hop(source, w, d, 0, pv, 256))


def travel(front, vectors, dofs, faces, mass):
    dma = pltpu.SemaphoreType.DMA
    return pl.pallas_call(
        travel_kernel,
        out_shape=(
            jax.ShapeDtypeStruct((512, 1024), F32),
            jax.ShapeDtypeStruct((1024, 1024), F32),
            jax.ShapeDtypeStruct((1024, 1024), F32),
            jax.ShapeDtypeStruct((64, 2048), F32),
        ),
        in_specs=[VM] * 5,
        out_specs=(ANY, ANY, ANY, VM),
        scratch_shapes=[
            pltpu.VMEM((64, 2304), F32),
            pltpu.VMEM((2, 64, 128), F32),
            pltpu.VMEM((24, 64, 128), F32),
            pltpu.VMEM((1024, 3072), BF16),
            pltpu.VMEM((256, 3072), BF16),
            dma((4, NSTEP)), dma((4, NSTEP)), dma((2, NSTEP)),
            dma((4,)), dma((4,)), dma((4,)), dma((4,)), dma((2,)), dma((2,)),
            dma((2,)), dma((2,)),
        ],
        compiler_params=pltpu.CompilerParams(collective_id=1, has_side_effects=True, vmem_limit_bytes=50 << 20),
    )(front, vectors, dofs, faces, mass)


def lanes(v, j):
    return jnp.broadcast_to(v[:, j : j + 1], (8, 128))


def subs(v, j):
    return jnp.broadcast_to(v[j : j + 1, :], (8, 128))


def tree(t):
    while len(t) > 1:
        t = [t[i] + t[i + 1] for i in range(0, len(t), 2)]
    return t[0]


def inverse8(cols, row8):
    cols = list(cols)
    for j in range(8):
        ip = 1.0 / subs(cols[j], j)
        pivot = cols[j]
        for m in range(8):
            if m != j:
                r = subs(cols[m], j) * ip
                cols[m] = jnp.where(row8 == j, r, cols[m] - pivot * r)
        cols[j] = jnp.where(row8 == j, ip, -pivot * ip)
    return cols


def inverse128(block):
    lane8 = lax.broadcasted_iota(jnp.int32, (8, 128), 1)
    row8 = lax.broadcasted_iota(jnp.int32, (8, 128), 0)
    v = [block[8 * i : 8 * i + 8] for i in range(16)]
    for kb in range(16):
        k0 = 8 * kb
        w = v[kb]
        cols = inverse8([lanes(w, k0 + j) for j in range(8)], row8)
        r = tree([cols[m] * subs(w, m) for m in range(8)])
        for m in range(8):
            r = jnp.where(lane8 == k0 + m, cols[m], r)
        rs = [subs(r, m) for m in range(8)]
        own = (lane8 // 8) == kb
        for i in list(range(kb + 1, 16)) + list(range(kb)):
            o = v[i]
            v[i] = jnp.where(own, 0.0, o) - tree([lanes(o, k0 + m) * rs[m] for m in range(8)])
        v[kb] = r
    return jnp.concatenate(v, 0)


def invert_in_place(ref):
    def body(b, _):
        s = pl.ds(pl.multiple_of(b * 128, 128), 128)
        d = inverse128(ref[s, s])
        c = ref[:, s]
        r = dot(d, ref[s, :])
        ref[...] = ref[...] - dot(c, r)
        ref[s, :] = r
        ref[:, s] = -dot(c, d)
        ref[s, s] = d
        return 0

    lax.fori_loop(0, 4, body, 0)


def update_kernel(bounds, diag, front, xr, rp, pv, out, a11, a12, a22, sem):
    row, col = lax.axis_index("row"), lax.axis_index("col")
    shift = (bounds[0] + bounds[1]).astype(F32) / 510.0

    def fetch(src):
        copies = [
            pltpu.make_async_copy(src.at[pl.ds(0, 512), pl.ds(0, 512)], a11, sem.at[0]),
            pltpu.make_async_copy(src.at[pl.ds(0, 512), pl.ds(512, 512)], a12, sem.at[1]),
            pltpu.make_async_copy(src.at[pl.ds(512, 512), pl.ds(512, 512)], a22, sem.at[2]),
        ]
        for c in copies:
            c.start()
        for c in copies:
            c.wait()

    @pl.when(col == 0)
    def _():
        fetch(rp)

    @pl.when(col > 0)
    def _():
        fetch(pv)

    ri = lax.broadcasted_iota(jnp.int32, (512, 512), 0)
    ci = lax.broadcasted_iota(jnp.int32, (512, 512), 1)
    a11[...] = a11[...] - jnp.where(ri == ci, shift * diag[:, 0:512], 0.0)
    a22[...] = a22[...] - jnp.where(ri == ci, shift * diag[:, 512:1024], 0.0)

    @pl.when((row == 0) & (col == 0))
    def _():
        out[:, 0:512] = a11[...]

    invert_in_place(a11)
    w = dot(a11[...], a12[...])
    s22 = a22[...] - dot(a12[...], w, TN)
    a12[...] = w
    a22[...] = s22

    @pl.when((row == 1) & (col == 0))
    def _():
        out[:, 0:512] = jnp.transpose(w)
        out[:, 512:1024] = s22

    @pl.when((row == 0) & (col == 0))
    def _():
        out[:, 512:1024] = w

    invert_in_place(a22)

    @pl.when(row >= 2)
    def _():
        x1, x2 = split(xr[:, 0:512]), xr[:, 512:1024]
        i2, ws = split(a22[...]), split(a12[...])
        l1 = dot3(x1, split(a11[...]))
        l2 = dot3(split(x2 - dot3(x1, ws)), i2)

        @pl.when(col == 0)
        def _():
            out[:, 0:512] = l1
            out[:, 512:1024] = l2

        @pl.when(col > 0)
        def _():
            l2s = split(l2)
            t1 = split(l1 - dot3(l2s, ws, NT))
            j = lax.broadcasted_iota(jnp.int32, (512, 1024), 1)
            i = lax.broadcasted_iota(jnp.int32, (512, 1024), 0)
            mine = diag[:, pl.ds(pl.multiple_of(col * 1024, 1024), 1024)]
            tile = front[...] - jnp.where(j + col * 1024 == i + row * 512, shift * mine, 0.0)
            out[...] = tile - dot3(t1, split(rp[0:512, :])) - dot3(l2s, split(rp[512:1024, :]))

    @pl.when((row == 0) & (col > 0))
    def _():
        out[...] = dot3(split(a11[...]), split(rp[0:512, :]))

    @pl.when((row == 1) & (col > 0))
    def _():
        out[...] = dot3(split(a22[...]), split(rp[512:1024, :] - dot3(split(a12[...]), split(rp[0:512, :]), TN)))


def update(bounds, diag, front, xr, rp, pv):
    return pl.pallas_call(
        update_kernel,
        out_shape=jax.ShapeDtypeStruct((512, 1024), F32),
        in_specs=[pl.BlockSpec(memory_space=pltpu.SMEM), VM, VM, VM, VM, ANY],
        out_specs=VM,
        scratch_shapes=[pltpu.VMEM((512, 512), F32)] * 3 + [pltpu.SemaphoreType.DMA((3,))],
        compiler_params=pltpu.CompilerParams(vmem_limit_bytes=56 << 20),
    )(bounds, diag, front, xr, rp, pv)


def lanczos_kernel(applied, basis, new, proj, chol, acc, slots, core_slot, send, recv):
    x, y, z, k = place()
    peers = [device(x + s, y, z, k) for s in (1, 2, 3)]
    peers += [device(x, y + s, z, k) for s in (1, 2, 3)]
    peers += [device(x, y, z + s, k) for s in (1, 2, 3)]
    peers += [device(x, y, z, 1 - k)]
    barrier = enter(peers)
    pl.semaphore_wait(barrier, len(peers))

    def reduce(phase, value):
        acc[phase, 0] = value
        c = remote(acc.at[phase, 0], core_slot.at[phase], send.at[phase, 9], recv.at[phase, 9], peers[9])
        c.start()
        c.wait()
        value = value + core_slot[phase]
        for axis, coordinate in enumerate((x, y, z)):
            acc[phase, axis + 1] = value
            copies = []
            for s in (1, 2, 3):
                n = 3 * axis + s - 1
                copies.append(
                    remote(
                        acc.at[phase, axis + 1], slots.at[phase, n], send.at[phase, n], recv.at[phase, n], peers[n]
                    )
                )
            for c in copies:
                c.start()
            for c in copies:
                c.wait()
            parts = [value] + [slots[phase, 3 * axis + s - 1] for s in (1, 2, 3)]
            ordered = []
            for q in range(4):
                away = (coordinate - q + 4) % 4
                part = parts[3]
                for s in (2, 1, 0):
                    part = jnp.where(away == s, parts[s], part)
                ordered.append(part)
            value = (ordered[0] + ordered[1]) + (ordered[2] + ordered[3])
        return value

    a = applied[...]
    pt = reduce(0, dot(a, basis[...], NT)) / TOTAL
    proj[...] = jnp.transpose(pt)
    corrected = a - dot(pt, basis[...])
    new[...] = corrected
    gram = dot(corrected, corrected, NT)
    gram = reduce(1, jnp.concatenate([gram, jnp.zeros((64, 64), F32)], axis=1)) / TOTAL

    lane8 = lax.broadcasted_iota(jnp.int32, (8, 128), 1)
    row8 = lax.broadcasted_iota(jnp.int32, (8, 128), 0)
    v = [gram[8 * i : 8 * i + 8] + jnp.where(lane8 == row8 + 64 + 8 * i, 1.0, 0.0) for i in range(8)]
    for kb in range(8):
        k0 = 8 * kb
        w = v[kb]
        first = [lanes(w, k0 + j) for j in range(8)]
        cols = inverse8(first, row8)
        r = tree([cols[m] * subs(w, m) for m in range(8)])
        rs = [subs(r, m) for m in range(8)]
        for i in range(kb + 1, 8):
            o = v[i]
            v[i] = o - tree([lanes(o, k0 + m) * rs[m] for m in range(8)])
        c = list(first)
        scale = jnp.zeros((8, 128), F32)
        for j in range(8):
            p = subs(c[j], j)
            f = jnp.where(row8 > j, c[j] / p, 0.0)
            w = w - f * subs(w, j)
            for m in range(j + 1, 8):
                c[m] = c[m] - f * subs(c[m], j)
            scale = jnp.where(row8 == j, p, scale)
        v[kb] = w / jnp.sqrt(scale)
    full = jnp.concatenate(v, 0)
    upper, inverse = full[:, 0:64], full[:, 64:128]
    ri = lax.broadcasted_iota(jnp.int32, (64, 64), 0)
    ci = lax.broadcasted_iota(jnp.int32, (64, 64), 1)
    chol[...] = jnp.transpose(jnp.where(ri <= ci, upper, 0.0))
    new[...] = dot(inverse, new[...])


def lanczos(applied, basis):
    dma = pltpu.SemaphoreType.DMA
    return pl.pallas_call(
        lanczos_kernel,
        out_shape=(
            jax.ShapeDtypeStruct((64, 2048), F32),
            jax.ShapeDtypeStruct((128, 64), F32),
            jax.ShapeDtypeStruct((64, 64), F32),
        ),
        in_specs=[VM, VM],
        out_specs=(VM, VM, VM),
        scratch_shapes=[
            pltpu.VMEM((2, 4, 64, 128), F32),
            pltpu.VMEM((2, 9, 64, 128), F32),
            pltpu.VMEM((2, 64, 128), F32),
            dma((2, 10)), dma((2, 10)),
        ],
        compiler_params=pltpu.CompilerParams(collective_id=2, has_side_effects=True, vmem_limit_bytes=40 << 20),
    )(applied, basis)


def shards(front, mass_diag, shift_bounds, vectors, basis, element_dofs, face_dofs, mass_blocks):
    xr, rp, pv, applied = travel(
        front, vectors, element_dofs.reshape(24, 1, 512), face_dofs.reshape(2, 1, 128), mass_blocks
    )
    new_block, projections, cholesky_factor = lanczos(applied, basis)
    factor = update(shift_bounds, mass_diag.reshape(1, -1), front, xr, rp, pv)
    return factor, new_block, projections, cholesky_factor


def solution(mesh):
    placed = (
        P("row", "col"),
        P(),
        P(),
        P(None, ("row", "col")),
        P(None, ("row", "col")),
        P(None, ("row", "col")),
        P(("row", "col"), None),
        P(None, None, ("row", "col")),
    )
    return jax.shard_map(
        shards,
        mesh=mesh,
        in_specs=placed,
        out_specs=(P("row", "col"), P(None, ("row", "col")), P(), P()),
        check_vma=False,
    )
```

```python
import functools

import jax
import jax.numpy as jnp
from jax import lax
from jax.experimental import pallas as pl
from jax.experimental.pallas import tpu as pltpu
from jax.sharding import PartitionSpec as P

MESH = pl.DeviceIdType.MESH
HI = lax.Precision.HIGHEST
F32 = jnp.float32
BF16 = jnp.bfloat16
STEP = 32
LAG = 2
NSTEP = 256 // STEP
TOTAL = 262144.0
VM = pl.BlockSpec(memory_space=pltpu.VMEM)
ANY = pl.BlockSpec(memory_space=pl.ANY)
NT = (((1,), (1,)), ((), ()))
NN = (((1,), (0,)), ((), ()))
TN = (((0,), (0,)), ((), ()))


def dot(a, b, dims=NN):
    return lax.dot_general(a, b, dims, precision=HI, preferred_element_type=F32)


def split(a):
    high = a.astype(BF16)
    return high, (a - high.astype(F32)).astype(BF16)


def dot3(a, b, dims=NN):
    (ah, al), (bh, bl) = a, b

    def one(l, r):
        return lax.dot_general(l, r, dims, preferred_element_type=F32)

    return one(ah, bh) + (one(ah, bl) + one(al, bh))


def place():
    row, col = lax.axis_index("row"), lax.axis_index("col")
    return row % 4, row // 4, col // 2, col % 2


def device(x, y, z, k):
    return ((y % 4) * 4 + (x % 4), (z % 4) * 2 + k)


def enter(peers):
    barrier = pltpu.get_barrier_semaphore()
    for peer in peers:
        pl.semaphore_signal(barrier, inc=1, device_id=peer, device_id_type=MESH)
    return barrier


def remote(src, dst, send, recv, peer):
    return pltpu.make_async_remote_copy(
        src_ref=src, dst_ref=dst, send_sem=send, recv_sem=recv, device_id=peer, device_id_type=MESH
    )


def lanes(v, j):
    return jnp.broadcast_to(v[:, j : j + 1], (8, 128))


def subs(v, j):
    return jnp.broadcast_to(v[j : j + 1, :], (8, 128))


def tree(t):
    while len(t) > 1:
        t = [t[i] + t[i + 1] for i in range(0, len(t), 2)]
    return t[0]


def inverse8(cols, row8):
    cols = list(cols)
    for j in range(8):
        ip = 1.0 / subs(cols[j], j)
        pivot = cols[j]
        for m in range(8):
            if m != j:
                r = subs(cols[m], j) * ip
                cols[m] = jnp.where(row8 == j, r, cols[m] - pivot * r)
        cols[j] = jnp.where(row8 == j, ip, -pivot * ip)
    return cols


def inverse128(block, between):
    lane8 = lax.broadcasted_iota(jnp.int32, (8, 128), 1)
    row8 = lax.broadcasted_iota(jnp.int32, (8, 128), 0)
    v = [block[8 * i : 8 * i + 8] for i in range(16)]
    for kb in range(16):
        if kb % 4 == 0:
            between(kb // 4)
        k0 = 8 * kb
        w = v[kb]
        cols = inverse8([lanes(w, k0 + j) for j in range(8)], row8)
        r = tree([cols[m] * subs(w, m) for m in range(8)])
        for m in range(8):
            r = jnp.where(lane8 == k0 + m, cols[m], r)
        rs = [subs(r, m) for m in range(8)]
        own = (lane8 // 8) == kb
        for i in list(range(kb + 1, 16)) + list(range(kb)):
            o = v[i]
            v[i] = jnp.where(own, 0.0, o) - tree([lanes(o, k0 + m) * rs[m] for m in range(8)])
        v[kb] = r
    return jnp.concatenate(v, 0)


def invert_in_place(ref, between, after):
    def body(b, _):
        s = pl.ds(pl.multiple_of(b * 128, 128), 128)
        d = inverse128(ref[s, s], functools.partial(between, b))
        c = ref[:, s]
        r = dot(d, ref[s, :])
        ref[...] = ref[...] - dot(c, r)
        ref[s, :] = r
        ref[:, s] = -dot(c, d)
        ref[s, s] = d
        after(b)
        return 0

    lax.fori_loop(0, 4, body, 0)


def pick(ext_ref, index, chunks):
    low = jnp.broadcast_to(index & 127, (64, 128))
    high = jnp.broadcast_to(index >> 7, (64, 128))
    found = jnp.take_along_axis(ext_ref[:, 0:128], low, axis=1)
    for c in range(1, chunks):
        found = jnp.where(high == c, jnp.take_along_axis(ext_ref[:, 128 * c : 128 * c + 128], low, axis=1), found)
    return found


def step_kernel(
    bounds, diag, vectors, dofs, faces, front, mass_hbm, basis_hbm,
    out, new, proj, chol,
    xr, rp, pv, applied, ext, fs, got, wide, hot, mass, basis, a11, a12, a22, acc, slots, core_slot,
    rp_in, pv_in, xr_in, rpx, rpy, pvz, pvc, xrz, xrc, face_out, face_in, load, send, recv,
):
    x, y, z, k = place()
    me = lax.axis_index("row") * 8 + lax.axis_index("col")
    before, after = (me + 127) % 128, (me + 1) % 128
    peers = [
        device(x + 1, y, z, k), device(x + 3, y, z, k), device(x, y + 1, z, k), device(x, y + 3, z, k),
        device(x, y, z + 1, k), device(x, y, z + 3, k), device(x, y, z, 1 - k),
        (before // 8, before % 8), (after // 8, after % 8),
        device(x + 2, y, z, k), device(x, y + 2, z, k), device(x, y, z + 2, k),
    ]
    barrier = enter(peers)
    on_x = [[lax.rem((x - source) * d + 8, 4) for d in (1, -1)] for source in range(2)]
    on_y = [lax.rem(y * d + 8, 4) for d in (1, -1)]
    on_z = [lax.rem(z * d + 8, 4) for d in (1, -1)]
    next_x, next_y, next_z = peers[0:2], peers[2:4], peers[4:6]
    other = peers[6]
    far_x = [[(y == 0) & (on_x[source][w] < 3) for w in range(2)] for source in range(2)]
    far_y = [on_y[w] < 3 for w in range(2)]
    far_z = [(k == 0) & (on_z[w] < 3) for w in range(2)]
    first_core = k == 0
    lag_xy = [[LAG * (on_x[source][w] + on_y[w]) for w in range(2)] for source in range(2)]
    lag_z = [LAG * (on_z[w] + k) for w in range(2)]

    def rows(ref, first, count=STEP):
        return ref.at[pl.ds(pl.multiple_of(first, STEP), count), :]

    def half(ref, first, count=STEP):
        return ref.at[pl.ds(pl.multiple_of(first, STEP), count), pl.ds(512, 512)]

    def ways():
        return ((0, 1), (1, -1))

    loads = [
        pltpu.make_async_copy(mass_hbm, mass, load.at[0]),
        pltpu.make_async_copy(basis_hbm, basis, load.at[1]),
        pltpu.make_async_copy(front, out, load.at[2]),
    ]
    for c in loads:
        c.start()

    origin = (z == 0) & (k == 0)

    def own_piece(source, view):
        for w, _ in ways():
            for i in range(NSTEP):
                own = 256 * w + STEP * i
                pltpu.make_async_copy(
                    view(front, own), view(rp, 512 * source + own), rp_in.at[2 * source + w, i]
                ).start()

    @pl.when((x == 0) & (y == 0))
    def _():
        own_piece(0, rows)

    @pl.when((x == 1) & (y == 0) & origin)
    def _():
        own_piece(1, half)

    @pl.when((x == 1) & (y == 0) & ~origin)
    def _():
        own_piece(1, rows)

    @pl.when((z == 0) & (k == 0))
    def _():
        for w, _ in ways():
            for i in range(NSTEP):
                own = 256 * w + STEP * i
                pltpu.make_async_copy(rows(front, own), rows(xr, own), xr_in.at[w, i]).start()

    ext[:, 0:2048] = vectors[...]
    fs[0] = pick(ext, faces[0], 16)
    fs[1] = pick(ext, faces[1], 16)

    @pl.when(me == 0)
    def _():
        ext[:, 2048:2176] = jnp.zeros((64, 128), F32)

    @pl.when(me == 127)
    def _():
        ext[:, 2176:2304] = jnp.zeros((64, 128), F32)

    pl.semaphore_wait(barrier, len(peers))

    to_before = remote(fs.at[0], ext.at[:, pl.ds(2176, 128)], face_out.at[0], face_in.at[0], (before // 8, before % 8))
    to_after = remote(fs.at[1], ext.at[:, pl.ds(2048, 128)], face_out.at[1], face_in.at[1], (after // 8, after % 8))

    @pl.when(me > 0)
    def _():
        to_before.start()

    @pl.when(me < 127)
    def _():
        to_after.start()

    def rp_hop(source, w, d, i, count=STEP, view=rows):
        n = 2 * source + w
        c = view(rp, 512 * source + 256 * w + STEP * i, count)
        return (
            remote(c, c, rpx.at[n], rp_in.at[n, i], next_x[w]), far_x[source][w],
            remote(c, c, rpy.at[n], rp_in.at[n, i], next_y[w]), far_y[w],
        )

    def pv_hop(source, w, d, i, src, count=STEP):
        n = 2 * source + w
        view = half if source else rows
        first = 512 * source + 256 * w + STEP * i
        return (
            remote(view(src, first, count), view(pv, first, count), pvz.at[n], pv_in.at[n, i], next_z[w]), far_z[w],
            remote(view(src, first, count), view(pv, first, count), pvc.at[n], pv_in.at[n, i], other), first_core,
        )

    def xr_hop(w, d, i, count=STEP):
        c = rows(xr, 256 * w + STEP * i, count)
        return (
            remote(c, c, xrz.at[w], xr_in.at[w, i], next_z[w]), far_z[w],
            remote(c, c, xrc.at[w], xr_in.at[w, i], other), first_core,
        )

    def pass_on(hop, received=True):
        one, p1, two, p2 = hop
        if received:
            one.wait_recv()

        @pl.when(p1)
        def _():
            one.start()

        @pl.when(p2)
        def _():
            two.start()

    def pivot_slot(t):
        for source in range(2):
            view = half if source else rows
            for w, d in ways():
                i = t - NSTEP * source - lag_xy[source][w]

                @pl.when(origin & (i >= 0) & (i < NSTEP))
                def _():
                    pass_on(rp_hop(source, w, d, i, STEP, view))
                    pass_on(pv_hop(source, w, d, i, rp), False)

                j = i - lag_z[w]

                @pl.when(~origin & (j >= 0) & (j < NSTEP))
                def _():
                    pass_on(pv_hop(source, w, d, j, pv))

    def panel_slot(t):
        for source in range(2):
            for w, d in ways():
                i = t - NSTEP * source - lag_xy[source][w]

                @pl.when(~origin & (i >= 0) & (i < NSTEP))
                def _():
                    pass_on(rp_hop(source, w, d, i))

        for w, d in ways():
            i = t - 12 - lag_z[w]

            @pl.when((i >= 0) & (i < NSTEP))
            def _():
                pass_on(xr_hop(w, d, i))

    def gather_hook(e, b):
        @pl.when(lax.rem(b, 6) == 0)
        def _():
            pivot_slot(7 * e + lax.div(b, 6))

        @pl.when(lax.rem(b, 12) == 3)
        def _():
            panel_slot(3 * e + lax.div(b, 12))

    def contract_hook(e, a4):
        @pl.when(lax.rem(a4, 2) == 0)
        def _():
            pivot_slot(7 * e + 4 + lax.div(a4, 2))

        @pl.when(a4 == 3)
        def _():
            panel_slot(3 * e + 2)

    @pl.when(me > 0)
    def _():
        to_before.wait_send()
        to_after.wait_recv()

    @pl.when(me < 127)
    def _():
        to_after.wait_send()
        to_before.wait_recv()

    applied[...] = jnp.zeros_like(applied)
    loads[0].wait()
    sub = lax.broadcasted_iota(jnp.int32, (256, 128), 0)

    def chunk(e, _):
        es = pl.ds(pl.multiple_of(e * 128, 128), 128)

        def gather(b, _):
            gather_hook(e, b)
            got[b] = pick(ext, dofs[b, :, es], 18)
            return 0

        lax.fori_loop(0, 24, gather, 0)

        def contract(a4, _):
            contract_hook(e, a4)
            total = [jnp.zeros((64, 128), F32) for _ in range(4)]
            for b in range(24):
                g = got[b]
                for q in range(4):
                    total[q] = total[q] + mass[a4 * 4 + q, pl.ds(b, 1), es] * g
            for q in range(4):
                a = a4 * 4 + q
                index = dofs[a, :, es]
                high = jnp.broadcast_to(index >> 8, (64, 128))
                low = jnp.broadcast_to(index & 255, (256, 128))
                big = total[q].astype(BF16).astype(F32)
                small = total[q] - big
                ps = pl.ds(pl.multiple_of(a * 128, 128), 128)
                for c in range(8):
                    here = high == c
                    wide[64 * c : 64 * c + 64, ps] = jnp.where(here, big, 0.0).astype(BF16)
                    wide[512 + 64 * c : 576 + 64 * c, ps] = jnp.where(here, small, 0.0).astype(BF16)
                hot[:, ps] = jnp.where(sub == low, 1.0, 0.0).astype(BF16)
            return 0

        lax.fori_loop(0, 6, contract, 0)
        out = lax.dot_general(wide[...], hot[...], NT, preferred_element_type=F32)
        for c in range(8):
            applied[:, 256 * c : 256 * c + 256] += out[64 * c : 64 * c + 64] + out[512 + 64 * c : 576 + 64 * c]
        return 0

    lax.fori_loop(0, 4, chunk, 0)

    lines = [device(x, y, z, 1 - k)]
    lines += [device(x + s, y, z, k) for s in (1, 2, 3)]
    lines += [device(x, y + s, z, k) for s in (1, 2, 3)]
    lines += [device(x, y, z + s, k) for s in (1, 2, 3)]

    def sum_copies(phase, stage):
        if stage == 0:
            return [remote(acc.at[phase, 0], core_slot.at[phase], send.at[phase, 0], recv.at[phase, 0], lines[0])]
        return [
            remote(acc.at[phase, stage], slots.at[phase, n - 1], send.at[phase, n], recv.at[phase, n], lines[n])
            for n in range(3 * stage - 2, 3 * stage + 1)
        ]

    def start_sum(phase, stage):
        for c in sum_copies(phase, stage):
            c.start()

    def finish_sum(phase, stage):
        for c in sum_copies(phase, stage):
            c.wait()
        value = acc[phase, stage]
        if stage == 0:
            acc[phase, 1] = value + core_slot[phase]
            return
        coordinate = (x, y, z)[stage - 1]
        parts = [value] + [slots[phase, 3 * stage - 4 + s] for s in (1, 2, 3)]
        ordered = []
        for q in range(4):
            away = (coordinate - q + 4) % 4
            part = parts[3]
            for s in (2, 1, 0):
                part = jnp.where(away == s, parts[s], part)
            ordered.append(part)
        acc[phase, stage + 1] = (ordered[0] + ordered[1]) + (ordered[2] + ordered[3])

    row, col = lax.axis_index("row"), lax.axis_index("col")
    shift = (bounds[0] + bounds[1]).astype(F32) / 510.0
    ri = lax.broadcasted_iota(jnp.int32, (512, 512), 0)
    ci = lax.broadcasted_iota(jnp.int32, (512, 512), 1)

    def pivot(ref, r, c, shifted):
        for where, src in ((col == 0, rp), (col > 0, pv)):
            @pl.when(where)
            def _():
                block = src[r : r + 512, c : c + 512]
                if shifted:
                    block = block - jnp.where(ri == ci, shift * diag[:, c : c + 512], 0.0)
                ref[...] = block

    loads[1].wait()
    acc[0, 0] = dot(applied[...], basis[...], NT)
    start_sum(0, 0)
    loads[2].wait()
    pivot(a11, 0, 0, True)

    @pl.when((row == 0) & (col == 0))
    def _():
        out[:, 0:512] = a11[...]

    def first_slots(b, q):
        if q % 2 == 0:
            pivot_slot(28 + 2 * b + q // 2)
        else:
            panel_slot(12 + 2 * b + q // 2)

    def last_slots(b, q):
        if q % 2 == 1:
            panel_slot(20 + 2 * b + q // 2)

    def advance(phase, b):
        for stage in range(4):
            @pl.when(b == stage)
            def _():
                finish_sum(phase, stage)
                if stage < 3:
                    start_sum(phase, stage + 1)

    invert_in_place(a11, first_slots, functools.partial(advance, 0))

    pt = acc[0, 4] / TOTAL
    proj[...] = jnp.transpose(pt)
    corrected = applied[...] - dot(pt, basis[...])
    applied[...] = corrected
    acc[1, 0] = jnp.concatenate([dot(corrected, corrected, NT), jnp.zeros((64, 64), F32)], axis=1)
    start_sum(1, 0)

    pivot(a12, 0, 512, False)
    pivot(a22, 512, 512, True)
    w = dot(a11[...], a12[...])
    s22 = a22[...] - dot(a12[...], w, TN)
    a12[...] = w
    a22[...] = s22

    @pl.when((row == 1) & (col == 0))
    def _():
        out[:, 0:512] = jnp.transpose(w)
        out[:, 512:1024] = s22

    @pl.when((row == 0) & (col == 0))
    def _():
        out[:, 512:1024] = w

    invert_in_place(a22, last_slots, functools.partial(advance, 1))

    @pl.when(row >= 2)
    def _():
        x1, x2 = split(xr[:, 0:512]), xr[:, 512:1024]
        i2, ws = split(a22[...]), split(a12[...])
        l1 = dot3(x1, split(a11[...]))
        l2 = dot3(split(x2 - dot3(x1, ws)), i2)

        @pl.when(col == 0)
        def _():
            out[:, 0:512] = l1
            out[:, 512:1024] = l2

        @pl.when(col > 0)
        def _():
            l2s = split(l2)
            t1 = split(l1 - dot3(l2s, ws, NT))
            j = lax.broadcasted_iota(jnp.int32, (512, 1024), 1)
            i = lax.broadcasted_iota(jnp.int32, (512, 1024), 0)
            mine = diag[:, pl.ds(pl.multiple_of(col * 1024, 1024), 1024)]
            tile = out[...] - jnp.where(j + col * 1024 == i + row * 512, shift * mine, 0.0)
            out[...] = tile - dot3(t1, split(rp[0:512, :])) - dot3(l2s, split(rp[512:1024, :]))

    @pl.when((row == 0) & (col > 0))
    def _():
        out[...] = dot3(split(a11[...]), split(rp[0:512, :]))

    @pl.when((row == 1) & (col > 0))
    def _():
        out[...] = dot3(split(a22[...]), split(rp[512:1024, :] - dot3(split(a12[...]), split(rp[0:512, :]), TN)))

    gram = acc[1, 4] / TOTAL
    lane8 = lax.broadcasted_iota(jnp.int32, (8, 128), 1)
    row8 = lax.broadcasted_iota(jnp.int32, (8, 128), 0)
    v = [gram[8 * i : 8 * i + 8] + jnp.where(lane8 == row8 + 64 + 8 * i, 1.0, 0.0) for i in range(8)]
    for kb in range(8):
        k0 = 8 * kb
        w = v[kb]
        first = [lanes(w, k0 + j) for j in range(8)]
        cols = inverse8(first, row8)
        r = tree([cols[m] * subs(w, m) for m in range(8)])
        rs = [subs(r, m) for m in range(8)]
        for i in range(kb + 1, 8):
            o = v[i]
            v[i] = o - tree([lanes(o, k0 + m) * rs[m] for m in range(8)])
        c = list(first)
        scale = jnp.zeros((8, 128), F32)
        for j in range(8):
            p = subs(c[j], j)
            f = jnp.where(row8 > j, c[j] / p, 0.0)
            w = w - f * subs(w, j)
            for m in range(j + 1, 8):
                c[m] = c[m] - f * subs(c[m], j)
            scale = jnp.where(row8 == j, p, scale)
        v[kb] = w / jnp.sqrt(scale)
    full = jnp.concatenate(v, 0)
    upper, inverse = full[:, 0:64], full[:, 64:128]
    ri = lax.broadcasted_iota(jnp.int32, (64, 64), 0)
    ci = lax.broadcasted_iota(jnp.int32, (64, 64), 1)
    chol[...] = jnp.transpose(jnp.where(ri <= ci, upper, 0.0))
    new[...] = dot(inverse, applied[...])

    def drain(hop):
        one, p1, two, p2 = hop

        @pl.when(p1)
        def _():
            one.wait_send()

        @pl.when(p2)
        def _():
            two.wait_send()

    for w, d in ways():
        drain(xr_hop(w, d, 0, 256))
        drain(rp_hop(0, w, d, 0, 256))

        @pl.when(origin)
        def _():
            drain(rp_hop(1, w, d, 0, 256, half))

        @pl.when(~origin)
        def _():
            drain(rp_hop(1, w, d, 0, 256))

        for source in range(2):
            drain(pv_hop(source, w, d, 0, pv, 256))


def step(bounds, diag, vectors, dofs, faces, front, mass, basis):
    dma = pltpu.SemaphoreType.DMA
    return pl.pallas_call(
        step_kernel,
        out_shape=(
            jax.ShapeDtypeStruct((512, 1024), F32),
            jax.ShapeDtypeStruct((64, 2048), F32),
            jax.ShapeDtypeStruct((128, 64), F32),
            jax.ShapeDtypeStruct((64, 64), F32),
        ),
        in_specs=[pl.BlockSpec(memory_space=pltpu.SMEM), VM, VM, VM, VM, ANY, ANY, ANY],
        out_specs=(VM, VM, VM, VM),
        scratch_shapes=[
            pltpu.VMEM((512, 1024), F32),
            pltpu.VMEM((1024, 1024), F32),
            pltpu.VMEM((1024, 1024), F32),
            pltpu.VMEM((64, 2048), F32),
            pltpu.VMEM((64, 2304), F32),
            pltpu.VMEM((2, 64, 128), F32),
            pltpu.VMEM((24, 64, 128), F32),
            pltpu.VMEM((1024, 3072), BF16),
            pltpu.VMEM((256, 3072), BF16),
            pltpu.VMEM((24, 24, 512), F32),
            pltpu.VMEM((128, 2048), F32),
            pltpu.VMEM((512, 512), F32),
            pltpu.VMEM((512, 512), F32),
            pltpu.VMEM((512, 512), F32),
            pltpu.VMEM((2, 5, 64, 128), F32),
            pltpu.VMEM((2, 9, 64, 128), F32),
            pltpu.VMEM((2, 64, 128), F32),
            dma((4, NSTEP)), dma((4, NSTEP)), dma((2, NSTEP)),
            dma((4,)), dma((4,)), dma((4,)), dma((4,)), dma((2,)), dma((2,)),
            dma((2,)), dma((2,)), dma((3,)), dma((2, 10)), dma((2, 10)),
        ],
        compiler_params=pltpu.CompilerParams(collective_id=1, has_side_effects=True, vmem_limit_bytes=60 << 20),
    )(bounds, diag, vectors, dofs, faces, front, mass, basis)


def shards(front, mass_diag, shift_bounds, vectors, basis, element_dofs, face_dofs, mass_blocks):
    return step(
        shift_bounds, mass_diag.reshape(1, -1), vectors,
        element_dofs.reshape(24, 1, 512), face_dofs.reshape(2, 1, 128), front, mass_blocks, basis,
    )


def solution(mesh):
    placed = (
        P("row", "col"),
        P(),
        P(),
        P(None, ("row", "col")),
        P(None, ("row", "col")),
        P(None, ("row", "col")),
        P(("row", "col"), None),
        P(None, None, ("row", "col")),
    )
    return jax.shard_map(
        shards,
        mesh=mesh,
        in_specs=placed,
        out_specs=(P("row", "col"), P(None, ("row", "col")), P(), P()),
        check_vma=False,
    )
```

```python
import functools

import jax
import jax.numpy as jnp
from jax import lax
from jax.experimental import pallas as pl
from jax.experimental.pallas import tpu as pltpu
from jax.sharding import PartitionSpec as P

MESH = pl.DeviceIdType.MESH
HI = lax.Precision.HIGHEST
F32 = jnp.float32
BF16 = jnp.bfloat16
STEP = 32
LAG = 2
NSTEP = 256 // STEP
TOTAL = 262144.0
VM = pl.BlockSpec(memory_space=pltpu.VMEM)
ANY = pl.BlockSpec(memory_space=pl.ANY)
NT = (((1,), (1,)), ((), ()))
NN = (((1,), (0,)), ((), ()))
TN = (((0,), (0,)), ((), ()))


def dot(a, b, dims=NN):
    return lax.dot_general(a, b, dims, precision=HI, preferred_element_type=F32)


def split(a):
    high = a.astype(BF16)
    return high, (a - high.astype(F32)).astype(BF16)


def dot3(a, b, dims=NN):
    (ah, al), (bh, bl) = a, b

    def one(l, r):
        return lax.dot_general(l, r, dims, preferred_element_type=F32)

    return one(ah, bh) + (one(ah, bl) + one(al, bh))


def place():
    row, col = lax.axis_index("row"), lax.axis_index("col")
    return row % 4, row // 4, col // 2, col % 2


def device(x, y, z, k):
    return ((y % 4) * 4 + (x % 4), (z % 4) * 2 + k)


def enter(peers):
    barrier = pltpu.get_barrier_semaphore()
    for peer in peers:
        pl.semaphore_signal(barrier, inc=1, device_id=peer, device_id_type=MESH)
    return barrier


def remote(src, dst, send, recv, peer):
    return pltpu.make_async_remote_copy(
        src_ref=src, dst_ref=dst, send_sem=send, recv_sem=recv, device_id=peer, device_id_type=MESH
    )


def lanes(v, j):
    return jnp.broadcast_to(v[:, j : j + 1], (8, 128))


def subs(v, j):
    return jnp.broadcast_to(v[j : j + 1, :], (8, 128))


def tree(t):
    while len(t) > 1:
        t = [t[i] + t[i + 1] for i in range(0, len(t), 2)]
    return t[0]


def inverse8(cols, row8):
    cols = list(cols)
    for j in range(8):
        ip = 1.0 / subs(cols[j], j)
        pivot = cols[j]
        for m in range(8):
            if m != j:
                r = subs(cols[m], j) * ip
                cols[m] = jnp.where(row8 == j, r, cols[m] - pivot * r)
        cols[j] = jnp.where(row8 == j, ip, -pivot * ip)
    return cols


def inverse128(block, between):
    lane8 = lax.broadcasted_iota(jnp.int32, (8, 128), 1)
    row8 = lax.broadcasted_iota(jnp.int32, (8, 128), 0)
    v = [block[8 * i : 8 * i + 8] for i in range(16)]
    for kb in range(16):
        if kb % 4 == 0:
            between(kb // 4)
        k0 = 8 * kb
        w = v[kb]
        cols = inverse8([lanes(w, k0 + j) for j in range(8)], row8)
        r = tree([cols[m] * subs(w, m) for m in range(8)])
        for m in range(8):
            r = jnp.where(lane8 == k0 + m, cols[m], r)
        rs = [subs(r, m) for m in range(8)]
        own = (lane8 // 8) == kb
        for i in list(range(kb + 1, 16)) + list(range(kb)):
            o = v[i]
            v[i] = jnp.where(own, 0.0, o) - tree([lanes(o, k0 + m) * rs[m] for m in range(8)])
        v[kb] = r
    return jnp.concatenate(v, 0)


def invert_in_place(ref, between, after):
    def body(b, _):
        s = pl.ds(pl.multiple_of(b * 128, 128), 128)
        d = inverse128(ref[s, s], functools.partial(between, b))
        c = ref[:, s]
        r = dot(d, ref[s, :])
        ref[...] = ref[...] - dot(c, r)
        ref[s, :] = r
        ref[:, s] = -dot(c, d)
        ref[s, s] = d
        after(b)
        return 0

    lax.fori_loop(0, 4, body, 0)


def pick(ext_ref, index, chunks):
    low = jnp.broadcast_to(index & 127, (64, 128))
    high = jnp.broadcast_to(index >> 7, (64, 128))
    found = jnp.take_along_axis(ext_ref[:, 0:128], low, axis=1)
    for c in range(1, chunks):
        found = jnp.where(high == c, jnp.take_along_axis(ext_ref[:, 128 * c : 128 * c + 128], low, axis=1), found)
    return found


def step_kernel(
    bounds, diag, vectors, dofs_in, faces, front, mass_hbm, basis_hbm,
    out, new, proj, chol,
    dofs, xr, rp, pv, applied, ext, fs, got, wide, hot, mass, basis, a11, a12, a22, acc, slots, core_slot,
    rp_in, pn_in, pnx, pny, pv_in, xr_in, rpx, rpy, pvz, pvc, xrz, xrc, face_out, face_in, load, send, recv,
):
    x, y, z, k = place()
    me = lax.axis_index("row") * 8 + lax.axis_index("col")
    before, after = (me + 127) % 128, (me + 1) % 128
    peers = [
        device(x + 1, y, z, k), device(x + 3, y, z, k), device(x, y + 1, z, k), device(x, y + 3, z, k),
        device(x, y, z + 1, k), device(x, y, z + 3, k), device(x, y, z, 1 - k),
        (before // 8, before % 8), (after // 8, after % 8),
        device(x + 2, y, z, k), device(x, y + 2, z, k), device(x, y, z + 2, k),
    ]
    barrier = enter(peers)
    on_x = [[lax.rem((x - source) * d + 8, 4) for d in (1, -1)] for source in range(2)]
    on_y = [lax.rem(y * d + 8, 4) for d in (1, -1)]
    on_z = [lax.rem(z * d + 8, 4) for d in (1, -1)]
    next_x, next_y, next_z = peers[0:2], peers[2:4], peers[4:6]
    other = peers[6]
    far_x = [[(y == 0) & (on_x[source][w] < 3) for w in range(2)] for source in range(2)]
    far_y = [on_y[w] < 3 for w in range(2)]
    far_z = [(k == 0) & (on_z[w] < 3) for w in range(2)]
    first_core = k == 0
    lag_xy = [[LAG * (on_x[source][w] + on_y[w]) for w in range(2)] for source in range(2)]
    late = [(y == 0) & (x != source) for source in range(2)]
    lag_yx = [[LAG * (on_x[source][w] + on_y[w] + jnp.where(late[source], 4, 0)) for w in range(2)] for source in range(2)]
    b_far_x = [[(y != 0) & (on_x[source][w] < 3) for w in range(2)] for source in range(2)]
    b_far_y = [
        [((x == source) & (on_y[w] < 3)) | ((x != source) & (on_y[w] == 3)) for w in range(2)] for source in range(2)
    ]
    lag_z = [LAG * (on_z[w] + k) for w in range(2)]

    def rows(ref, first, count=STEP):
        return ref.at[pl.ds(pl.multiple_of(first, 16), count), :]

    def half(ref, first, count=STEP):
        return ref.at[pl.ds(pl.multiple_of(first, 16), count), pl.ds(512, 512)]

    def ways():
        return ((0, 1), (1, -1))

    loads = [
        pltpu.make_async_copy(mass_hbm, mass, load.at[0]),
        pltpu.make_async_copy(basis_hbm, basis, load.at[1]),
        pltpu.make_async_copy(front, out, load.at[2]),
    ]
    for c in loads:
        c.start()

    origin = (z == 0) & (k == 0)

    def own_piece(source, view):
        for w, _ in ways():
            for i in range(NSTEP):
                own = 256 * w + STEP * i
                pltpu.make_async_copy(
                    view(front, own), view(rp, 512 * source + own), rp_in.at[2 * source + w, i]
                ).start()

    def own_panel(source):
        for w, _ in ways():
            for i in range(16):
                own = 256 * w + 16 * i
                pltpu.make_async_copy(
                    rows(front, own, 16), rows(rp, 512 * source + own, 16), pn_in.at[2 * source + w, i]
                ).start()

    @pl.when((x == 0) & (y == 0) & origin)
    def _():
        own_piece(0, rows)

    @pl.when((x == 1) & (y == 0) & origin)
    def _():
        own_piece(1, half)

    @pl.when((x == 0) & (y == 0) & ~origin)
    def _():
        own_panel(0)

    @pl.when((x == 1) & (y == 0) & ~origin)
    def _():
        own_panel(1)

    @pl.when((z == 0) & (k == 0))
    def _():
        for w, _ in ways():
            for i in range(NSTEP):
                own = 256 * w + STEP * i
                pltpu.make_async_copy(rows(front, own), rows(xr, own), xr_in.at[w, i]).start()

    ext[:, 0:2048] = vectors[...]
    fs[0] = pick(ext, faces[0:1, :], 16)
    fs[1] = pick(ext, faces[1:2, :], 16)
    for b in range(24):
        dofs[b] = dofs_in[b : b + 1, :]

    @pl.when(me == 0)
    def _():
        ext[:, 2048:2176] = jnp.zeros((64, 128), F32)

    @pl.when(me == 127)
    def _():
        ext[:, 2176:2304] = jnp.zeros((64, 128), F32)

    pl.semaphore_wait(barrier, len(peers))

    to_before = remote(fs.at[0], ext.at[:, pl.ds(2176, 128)], face_out.at[0], face_in.at[0], (before // 8, before % 8))
    to_after = remote(fs.at[1], ext.at[:, pl.ds(2048, 128)], face_out.at[1], face_in.at[1], (after // 8, after % 8))

    @pl.when(me > 0)
    def _():
        to_before.start()

    @pl.when(me < 127)
    def _():
        to_after.start()

    def rp_hop(source, w, d, i, count=STEP, view=rows):
        n = 2 * source + w
        c = view(rp, 512 * source + 256 * w + STEP * i, count)
        return (
            remote(c, c, rpx.at[n], rp_in.at[n, i], next_x[w]), far_x[source][w],
            remote(c, c, rpy.at[n], rp_in.at[n, i], next_y[w]), far_y[w],
        )

    def panel_hop(source, w, kind, i, count=16):
        n = 2 * source + w
        c = rows(rp, 512 * source + 256 * w + 128 * kind + 16 * i, count)
        return (
            remote(c, c, pnx.at[n + 4 * kind], pn_in.at[n, i + 8 * kind], next_x[w]),
            b_far_x[source][w] if kind else far_x[source][w],
            remote(c, c, pny.at[n + 4 * kind], pn_in.at[n, i + 8 * kind], next_y[w]),
            b_far_y[source][w] if kind else far_y[w],
        )

    def pv_hop(source, w, d, i, src, count=STEP):
        n = 2 * source + w
        view = half if source else rows
        first = 512 * source + 256 * w + STEP * i
        return (
            remote(view(src, first, count), view(pv, first, count), pvz.at[n], pv_in.at[n, i], next_z[w]), far_z[w],
            remote(view(src, first, count), view(pv, first, count), pvc.at[n], pv_in.at[n, i], other), first_core,
        )

    def xr_hop(w, d, i, count=STEP):
        c = rows(xr, 256 * w + STEP * i, count)
        return (
            remote(c, c, xrz.at[w], xr_in.at[w, i], next_z[w]), far_z[w],
            remote(c, c, xrc.at[w], xr_in.at[w, i], other), first_core,
        )

    def pass_on(hop, received=True):
        one, p1, two, p2 = hop
        if received:
            one.wait_recv()

        @pl.when(p1)
        def _():
            one.start()

        @pl.when(p2)
        def _():
            two.start()

    def pivot_slot(t):
        for source in range(2):
            view = half if source else rows
            for w, d in ways():
                i = t - NSTEP * source - lag_xy[source][w]

                @pl.when(origin & (i >= 0) & (i < NSTEP))
                def _():
                    pass_on(rp_hop(source, w, d, i, STEP, view))
                    pass_on(pv_hop(source, w, d, i, rp), False)

                j = i - lag_z[w]

                @pl.when(~origin & (j >= 0) & (j < NSTEP))
                def _():
                    pass_on(pv_hop(source, w, d, j, pv))

    def panel_slot(t):
        for source in range(2):
            for w, _ in ways():
                for kind, lag in ((0, lag_xy[source][w]), (1, lag_yx[source][w])):
                    i = t - 8 * source - lag

                    @pl.when(~origin & (i >= 0) & (i < 8))
                    def _():
                        pass_on(panel_hop(source, w, kind, i))

        for w, d in ways():
            i = t - 14 - lag_z[w]

            @pl.when((i >= 0) & (i < NSTEP))
            def _():
                pass_on(xr_hop(w, d, i))

    def gather_hook(e, b):
        @pl.when(lax.rem(b, 6) == 0)
        def _():
            pivot_slot(7 * e + lax.div(b, 6))

        @pl.when(lax.rem(b, 12) == 3)
        def _():
            panel_slot(4 * e + lax.div(b, 12))

    def contract_hook(e, a4):
        @pl.when(lax.rem(a4, 2) == 0)
        def _():
            pivot_slot(7 * e + 4 + lax.div(a4, 2))

        @pl.when((a4 == 1) | (a4 == 3))
        def _():
            panel_slot(4 * e + 2 + lax.div(a4, 2))

    @pl.when(me > 0)
    def _():
        to_before.wait_send()
        to_after.wait_recv()

    @pl.when(me < 127)
    def _():
        to_after.wait_send()
        to_before.wait_recv()

    applied[...] = jnp.zeros_like(applied)
    loads[0].wait()
    sub = lax.broadcasted_iota(jnp.int32, (256, 128), 0)

    def chunk(e, _):
        es = pl.ds(pl.multiple_of(e * 128, 128), 128)

        def gather(b, _):
            gather_hook(e, b)
            got[b] = pick(ext, dofs[b, :, es], 18)
            return 0

        lax.fori_loop(0, 24, gather, 0)

        def contract(a4, _):
            contract_hook(e, a4)
            total = [jnp.zeros((64, 128), F32) for _ in range(4)]
            for b in range(24):
                g = got[b]
                for q in range(4):
                    total[q] = total[q] + mass[a4 * 4 + q, pl.ds(b, 1), es] * g
            for q in range(4):
                a = a4 * 4 + q
                index = dofs[a, :, es]
                high = jnp.broadcast_to(index >> 8, (64, 128))
                low = jnp.broadcast_to(index & 255, (256, 128))
                big = total[q].astype(BF16).astype(F32)
                small = total[q] - big
                ps = pl.ds(pl.multiple_of(a * 128, 128), 128)
                for c in range(8):
                    here = high == c
                    wide[64 * c : 64 * c + 64, ps] = jnp.where(here, big, 0.0).astype(BF16)
                    wide[512 + 64 * c : 576 + 64 * c, ps] = jnp.where(here, small, 0.0).astype(BF16)
                hot[:, ps] = jnp.where(sub == low, 1.0, 0.0).astype(BF16)
            return 0

        lax.fori_loop(0, 6, contract, 0)
        out = lax.dot_general(wide[...], hot[...], NT, preferred_element_type=F32)
        for c in range(8):
            applied[:, 256 * c : 256 * c + 256] += out[64 * c : 64 * c + 64] + out[512 + 64 * c : 576 + 64 * c]
        return 0

    lax.fori_loop(0, 4, chunk, 0)

    lines = [device(x, y, z, 1 - k)]
    lines += [device(x + s, y, z, k) for s in (1, 2, 3)]
    lines += [device(x, y + s, z, k) for s in (1, 2, 3)]
    lines += [device(x, y, z + s, k) for s in (1, 2, 3)]

    def sum_copies(phase, stage):
        if stage == 0:
            return [remote(acc.at[phase, 0], core_slot.at[phase], send.at[phase, 0], recv.at[phase, 0], lines[0])]
        return [
            remote(acc.at[phase, stage], slots.at[phase, n - 1], send.at[phase, n], recv.at[phase, n], lines[n])
            for n in range(3 * stage - 2, 3 * stage + 1)
        ]

    def start_sum(phase, stage):
        for c in sum_copies(phase, stage):
            c.start()

    def finish_sum(phase, stage):
        for c in sum_copies(phase, stage):
            c.wait()
        value = acc[phase, stage]
        if stage == 0:
            acc[phase, 1] = value + core_slot[phase]
            return
        coordinate = (x, y, z)[stage - 1]
        parts = [value] + [slots[phase, 3 * stage - 4 + s] for s in (1, 2, 3)]
        ordered = []
        for q in range(4):
            away = (coordinate - q + 4) % 4
            part = parts[3]
            for s in (2, 1, 0):
                part = jnp.where(away == s, parts[s], part)
            ordered.append(part)
        acc[phase, stage + 1] = (ordered[0] + ordered[1]) + (ordered[2] + ordered[3])

    row, col = lax.axis_index("row"), lax.axis_index("col")
    shift = (bounds[0] + bounds[1]).astype(F32) / 510.0
    ri = lax.broadcasted_iota(jnp.int32, (512, 512), 0)
    ci = lax.broadcasted_iota(jnp.int32, (512, 512), 1)

    def pivot(ref, r, c, shifted):
        for where, src in ((col == 0, rp), (col > 0, pv)):
            @pl.when(where)
            def _():
                block = src[r : r + 512, c : c + 512]
                if shifted:
                    block = block - jnp.where(ri == ci, shift * diag[:, c : c + 512], 0.0)
                ref[...] = block

    loads[1].wait()
    acc[0, 0] = dot(applied[...], basis[...], NT)
    start_sum(0, 0)
    loads[2].wait()
    pivot(a11, 0, 0, True)

    @pl.when((row == 0) & (col == 0))
    def _():
        out[:, 0:512] = a11[...]

    def first_slots(b, q):
        if q % 2 == 0:
            pivot_slot(28 + 2 * b + q // 2)
        else:
            panel_slot(16 + 2 * b + q // 2)

    def last_slots(b, q):
        if q % 2 == 1:
            panel_slot(24 + 2 * b + q // 2)

    def advance(phase, b):
        for stage in range(4):
            @pl.when(b == stage)
            def _():
                finish_sum(phase, stage)
                if stage < 3:
                    start_sum(phase, stage + 1)

    invert_in_place(a11, first_slots, functools.partial(advance, 0))

    pt = acc[0, 4] / TOTAL
    proj[...] = pt
    corrected = applied[...] - dot(pt, basis[...])
    applied[...] = corrected
    acc[1, 0] = jnp.concatenate([dot(corrected, corrected, NT), jnp.zeros((64, 64), F32)], axis=1)
    start_sum(1, 0)

    pivot(a12, 0, 512, False)
    pivot(a22, 512, 512, True)
    w = dot(a11[...], a12[...])
    s22 = a22[...] - dot(a12[...], w, TN)
    a12[...] = w
    a22[...] = s22

    @pl.when((row == 1) & (col == 0))
    def _():
        out[:, 0:512] = jnp.transpose(w)
        out[:, 512:1024] = s22

    @pl.when((row == 0) & (col == 0))
    def _():
        out[:, 512:1024] = w

    invert_in_place(a22, last_slots, functools.partial(advance, 1))

    @pl.when(row >= 2)
    def _():
        x1, x2 = split(xr[:, 0:512]), xr[:, 512:1024]
        i2, ws = split(a22[...]), split(a12[...])
        l1 = dot3(x1, split(a11[...]))
        l2 = dot3(split(x2 - dot3(x1, ws)), i2)

        @pl.when(col == 0)
        def _():
            out[:, 0:512] = l1
            out[:, 512:1024] = l2

        @pl.when(col > 0)
        def _():
            l2s = split(l2)
            t1 = split(l1 - dot3(l2s, ws, NT))
            j = lax.broadcasted_iota(jnp.int32, (512, 1024), 1)
            i = lax.broadcasted_iota(jnp.int32, (512, 1024), 0)
            mine = diag[:, pl.ds(pl.multiple_of(col * 1024, 1024), 1024)]
            tile = out[...] - jnp.where(j + col * 1024 == i + row * 512, shift * mine, 0.0)
            out[...] = tile - dot3(t1, split(rp[0:512, :])) - dot3(l2s, split(rp[512:1024, :]))

    @pl.when((row == 0) & (col > 0))
    def _():
        out[...] = dot3(split(a11[...]), split(rp[0:512, :]))

    @pl.when((row == 1) & (col > 0))
    def _():
        out[...] = dot3(split(a22[...]), split(rp[512:1024, :] - dot3(split(a12[...]), split(rp[0:512, :]), TN)))

    gram = acc[1, 4] / TOTAL
    lane8 = lax.broadcasted_iota(jnp.int32, (8, 128), 1)
    row8 = lax.broadcasted_iota(jnp.int32, (8, 128), 0)
    v = [gram[8 * i : 8 * i + 8] + jnp.where(lane8 == row8 + 64 + 8 * i, 1.0, 0.0) for i in range(8)]
    for kb in range(8):
        k0 = 8 * kb
        w = v[kb]
        first = [lanes(w, k0 + j) for j in range(8)]
        cols = inverse8(first, row8)
        r = tree([cols[m] * subs(w, m) for m in range(8)])
        rs = [subs(r, m) for m in range(8)]
        for i in range(kb + 1, 8):
            o = v[i]
            v[i] = o - tree([lanes(o, k0 + m) * rs[m] for m in range(8)])
        c = list(first)
        scale = jnp.zeros((8, 128), F32)
        for j in range(8):
            p = subs(c[j], j)
            f = jnp.where(row8 > j, c[j] / p, 0.0)
            w = w - f * subs(w, j)
            for m in range(j + 1, 8):
                c[m] = c[m] - f * subs(c[m], j)
            scale = jnp.where(row8 == j, p, scale)
        v[kb] = w / jnp.sqrt(scale)
    full = jnp.concatenate(v, 0)
    upper, inverse = full[:, 0:64], full[:, 64:128]
    ri = lax.broadcasted_iota(jnp.int32, (64, 64), 0)
    ci = lax.broadcasted_iota(jnp.int32, (64, 64), 1)
    chol[...] = jnp.transpose(jnp.where(ri <= ci, upper, 0.0))
    new[...] = dot(inverse, applied[...])

    def drain(hop):
        one, p1, two, p2 = hop

        @pl.when(p1)
        def _():
            one.wait_send()

        @pl.when(p2)
        def _():
            two.wait_send()

    for w, d in ways():
        drain(xr_hop(w, d, 0, 256))

        @pl.when(origin)
        def _():
            drain(rp_hop(0, w, d, 0, 256))
            drain(rp_hop(1, w, d, 0, 256, half))

        @pl.when(~origin)
        def _():
            for source in range(2):
                for kind in range(2):
                    drain(panel_hop(source, w, kind, 0, 128))

        for source in range(2):
            drain(pv_hop(source, w, d, 0, pv, 256))


def step(bounds, diag, vectors, dofs, faces, front, mass, basis):
    dma = pltpu.SemaphoreType.DMA
    return pl.pallas_call(
        step_kernel,
        out_shape=(
            jax.ShapeDtypeStruct((512, 1024), F32),
            jax.ShapeDtypeStruct((64, 2048), F32),
            jax.ShapeDtypeStruct((64, 128), F32),
            jax.ShapeDtypeStruct((64, 64), F32),
        ),
        in_specs=[pl.BlockSpec(memory_space=pltpu.SMEM), VM, VM, VM, VM, ANY, ANY, ANY],
        out_specs=(VM, VM, VM, VM),
        scratch_shapes=[
            pltpu.VMEM((24, 1, 512), jnp.int32),
            pltpu.VMEM((512, 1024), F32),
            pltpu.VMEM((1024, 1024), F32),
            pltpu.VMEM((1024, 1024), F32),
            pltpu.VMEM((64, 2048), F32),
            pltpu.VMEM((64, 2304), F32),
            pltpu.VMEM((2, 64, 128), F32),
            pltpu.VMEM((24, 64, 128), F32),
            pltpu.VMEM((1024, 3072), BF16),
            pltpu.VMEM((256, 3072), BF16),
            pltpu.VMEM((24, 24, 512), F32),
            pltpu.VMEM((128, 2048), F32),
            pltpu.VMEM((512, 512), F32),
            pltpu.VMEM((512, 512), F32),
            pltpu.VMEM((512, 512), F32),
            pltpu.VMEM((2, 5, 64, 128), F32),
            pltpu.VMEM((2, 9, 64, 128), F32),
            pltpu.VMEM((2, 64, 128), F32),
            dma((4, NSTEP)), dma((4, 16)), dma((8,)), dma((8,)), dma((4, NSTEP)), dma((2, NSTEP)),
            dma((4,)), dma((4,)), dma((4,)), dma((4,)), dma((2,)), dma((2,)),
            dma((2,)), dma((2,)), dma((3,)), dma((2, 10)), dma((2, 10)),
        ],
        compiler_params=pltpu.CompilerParams(collective_id=1, has_side_effects=True, vmem_limit_bytes=60 << 20),
    )(bounds, diag, vectors, dofs, faces, front, mass, basis)


def shards(front, mass_diag, shift_bounds, vectors, basis, element_dofs, face_dofs, mass_blocks):
    factor, new_block, projections, cholesky_factor = step(
        shift_bounds, mass_diag.reshape(1, -1), vectors,
        element_dofs, face_dofs, front, mass_blocks, basis,
    )
    return factor, new_block, projections.T, cholesky_factor


def solution(mesh):
    placed = (
        P("row", "col"),
        P(),
        P(),
        P(None, ("row", "col")),
        P(None, ("row", "col")),
        P(None, ("row", "col")),
        P(("row", "col"), None),
        P(None, None, ("row", "col")),
    )
    return jax.shard_map(
        shards,
        mesh=mesh,
        in_specs=placed,
        out_specs=(P("row", "col"), P(None, ("row", "col")), P(), P()),
        check_vma=False,
    )
```

```python
import functools

import jax
import jax.numpy as jnp
from jax import lax
from jax.experimental import pallas as pl
from jax.experimental.pallas import tpu as pltpu
from jax.sharding import PartitionSpec as P

MESH = pl.DeviceIdType.MESH
HI = lax.Precision.HIGHEST
F32 = jnp.float32
BF16 = jnp.bfloat16
STEP = 32
LAG = 2
NSTEP = 256 // STEP
TOTAL = 262144.0
VM = pl.BlockSpec(memory_space=pltpu.VMEM)
ANY = pl.BlockSpec(memory_space=pl.ANY)
NT = (((1,), (1,)), ((), ()))
NN = (((1,), (0,)), ((), ()))
TN = (((0,), (0,)), ((), ()))


def dot(a, b, dims=NN):
    return lax.dot_general(a, b, dims, precision=HI, preferred_element_type=F32)


def split(a):
    high = a.astype(BF16)
    return high, (a - high.astype(F32)).astype(BF16)


def dot3(a, b, dims=NN):
    (ah, al), (bh, bl) = a, b

    def one(l, r):
        return lax.dot_general(l, r, dims, preferred_element_type=F32)

    return one(ah, bh) + (one(ah, bl) + one(al, bh))


def place():
    row, col = lax.axis_index("row"), lax.axis_index("col")
    return row % 4, row // 4, col // 2, col % 2


def device(x, y, z, k):
    return ((y % 4) * 4 + (x % 4), (z % 4) * 2 + k)


def enter(peers):
    barrier = pltpu.get_barrier_semaphore()
    for peer in peers:
        pl.semaphore_signal(barrier, inc=1, device_id=peer, device_id_type=MESH)
    return barrier


def remote(src, dst, send, recv, peer):
    return pltpu.make_async_remote_copy(
        src_ref=src, dst_ref=dst, send_sem=send, recv_sem=recv, device_id=peer, device_id_type=MESH
    )


def lanes(v, j):
    return jnp.broadcast_to(v[:, j : j + 1], (8, 128))


def subs(v, j):
    return jnp.broadcast_to(v[j : j + 1, :], (8, 128))


def tree(t):
    while len(t) > 1:
        t = [t[i] + t[i + 1] for i in range(0, len(t), 2)]
    return t[0]


def inverse8(cols, row8):
    cols = list(cols)
    for j in range(8):
        ip = 1.0 / subs(cols[j], j)
        pivot = cols[j]
        for m in range(8):
            if m != j:
                r = subs(cols[m], j) * ip
                cols[m] = jnp.where(row8 == j, r, cols[m] - pivot * r)
        cols[j] = jnp.where(row8 == j, ip, -pivot * ip)
    return cols


def inverse128(block, between):
    lane8 = lax.broadcasted_iota(jnp.int32, (8, 128), 1)
    row8 = lax.broadcasted_iota(jnp.int32, (8, 128), 0)
    v = [block[8 * i : 8 * i + 8] for i in range(16)]
    for kb in range(16):
        if kb % 4 == 0:
            between(kb // 4)
        k0 = 8 * kb
        w = v[kb]
        cols = inverse8([lanes(w, k0 + j) for j in range(8)], row8)
        r = tree([cols[m] * subs(w, m) for m in range(8)])
        for m in range(8):
            r = jnp.where(lane8 == k0 + m, cols[m], r)
        rs = [subs(r, m) for m in range(8)]
        own = (lane8 // 8) == kb
        for i in list(range(kb + 1, 16)) + list(range(kb)):
            o = v[i]
            v[i] = jnp.where(own, 0.0, o) - tree([lanes(o, k0 + m) * rs[m] for m in range(8)])
        v[kb] = r
    return jnp.concatenate(v, 0)


def invert_in_place(ref, between, after):
    def body(b, _):
        s = pl.ds(pl.multiple_of(b * 128, 128), 128)
        d = inverse128(ref[s, s], functools.partial(between, b))
        c = ref[:, s]
        r = dot(d, ref[s, :])
        ref[...] = ref[...] - dot(c, r)
        ref[s, :] = r
        ref[:, s] = -dot(c, d)
        ref[s, s] = d
        after(b)
        return 0

    lax.fori_loop(0, 4, body, 0)


def pick(ext_ref, index, chunks):
    low = jnp.broadcast_to(index & 127, (64, 128))
    high = jnp.broadcast_to(index >> 7, (64, 128))
    found = jnp.take_along_axis(ext_ref[:, 0:128], low, axis=1)
    for c in range(1, chunks):
        found = jnp.where(high == c, jnp.take_along_axis(ext_ref[:, 128 * c : 128 * c + 128], low, axis=1), found)
    return found


def step_kernel(
    bounds, diag, vectors, dofs_in, faces, front, mass_hbm, basis_hbm,
    out, new, proj, chol,
    dofs, xr, rp, pv, applied, ext, fs, got, wide, hot, mass, basis, a11, a12, a22, acc, slots, core_slot,
    rp_in, pn_in, pnx, pny, pv_in, xr_in, rpx, rpy, pvz, pvc, xrz, xrc, face_out, face_in, load, send, recv,
):
    x, y, z, k = place()
    me = lax.axis_index("row") * 8 + lax.axis_index("col")
    before, after = (me + 127) % 128, (me + 1) % 128
    peers = [
        device(x + 1, y, z, k), device(x + 3, y, z, k), device(x, y + 1, z, k), device(x, y + 3, z, k),
        device(x, y, z + 1, k), device(x, y, z + 3, k), device(x, y, z, 1 - k),
        (before // 8, before % 8), (after // 8, after % 8),
        device(x + 2, y, z, k), device(x, y + 2, z, k), device(x, y, z + 2, k),
    ]
    barrier = enter(peers)
    on_x = [[lax.rem((x - source) * d + 8, 4) for d in (1, -1)] for source in range(2)]
    on_y = [lax.rem(y * d + 8, 4) for d in (1, -1)]
    on_z = [lax.rem(z * d + 8, 4) for d in (1, -1)]
    next_x, next_y, next_z = peers[0:2], peers[2:4], peers[4:6]
    other = peers[6]
    far_x = [[(y == 0) & (on_x[source][w] < 3) for w in range(2)] for source in range(2)]
    far_y = [on_y[w] < 3 for w in range(2)]
    far_z = [(k == 0) & (on_z[w] < 3) for w in range(2)]
    first_core = k == 0
    lag_xy = [[LAG * (on_x[source][w] + on_y[w]) for w in range(2)] for source in range(2)]
    late = [(y == 0) & (x != source) for source in range(2)]
    lag_yx = [[LAG * (on_x[source][w] + on_y[w] + jnp.where(late[source], 4, 0)) for w in range(2)] for source in range(2)]
    side = [(y != 0) & (x == source) for source in range(2)]
    lag_a = [[LAG * (on_x[source][w] + on_y[w] + jnp.where(side[source], 4, 0)) for w in range(2)] for source in range(2)]
    a_far_x = [
        [((y == 0) & (on_x[source][w] < 3)) | ((y != 0) & (on_x[source][w] == 3)) for w in range(2)] for source in range(2)
    ]
    a_far_y = [[(x != source) & (on_y[w] < 3) for w in range(2)] for source in range(2)]
    b_far_x = [[(y != 0) & (on_x[source][w] < 3) for w in range(2)] for source in range(2)]
    b_far_y = [
        [((x == source) & (on_y[w] < 3)) | ((x != source) & (on_y[w] == 3)) for w in range(2)] for source in range(2)
    ]
    lag_z = [LAG * (on_z[w] + k) for w in range(2)]

    def rows(ref, first, count=STEP):
        return ref.at[pl.ds(pl.multiple_of(first, 16), count), :]

    def half(ref, first, count=STEP):
        return ref.at[pl.ds(pl.multiple_of(first, 16), count), pl.ds(512, 512)]

    def ways():
        return ((0, 1), (1, -1))

    loads = [
        pltpu.make_async_copy(mass_hbm, mass, load.at[0]),
        pltpu.make_async_copy(basis_hbm, basis, load.at[1]),
        pltpu.make_async_copy(front, out, load.at[2]),
    ]
    for c in loads:
        c.start()

    origin = (z == 0) & (k == 0)

    def own_piece(source, view):
        for w, _ in ways():
            for i in range(NSTEP):
                own = 256 * w + STEP * i
                pltpu.make_async_copy(
                    view(front, own), view(rp, 512 * source + own), rp_in.at[2 * source + w, i]
                ).start()

    def own_panel(source):
        for w, _ in ways():
            for i in range(16):
                own = 256 * w + 16 * i
                pltpu.make_async_copy(
                    rows(front, own, 16), rows(rp, 512 * source + own, 16), pn_in.at[2 * source + w, i]
                ).start()

    @pl.when((x == 0) & (y == 0) & origin)
    def _():
        own_piece(0, rows)

    @pl.when((x == 1) & (y == 0) & origin)
    def _():
        own_piece(1, half)

    @pl.when((x == 0) & (y == 0) & ~origin)
    def _():
        own_panel(0)

    @pl.when((x == 1) & (y == 0) & ~origin)
    def _():
        own_panel(1)

    @pl.when((z == 0) & (k == 0))
    def _():
        for w, _ in ways():
            for i in range(NSTEP):
                own = 256 * w + STEP * i
                pltpu.make_async_copy(rows(front, own), rows(xr, own), xr_in.at[w, i]).start()

    ext[:, 0:2048] = vectors[...]
    fs[0] = pick(ext, faces[0:1, :], 16)
    fs[1] = pick(ext, faces[1:2, :], 16)
    for b in range(24):
        dofs[b] = dofs_in[b : b + 1, :]

    @pl.when(me == 0)
    def _():
        ext[:, 2048:2176] = jnp.zeros((64, 128), F32)

    @pl.when(me == 127)
    def _():
        ext[:, 2176:2304] = jnp.zeros((64, 128), F32)

    pl.semaphore_wait(barrier, len(peers))

    to_before = remote(fs.at[0], ext.at[:, pl.ds(2176, 128)], face_out.at[0], face_in.at[0], (before // 8, before % 8))
    to_after = remote(fs.at[1], ext.at[:, pl.ds(2048, 128)], face_out.at[1], face_in.at[1], (after // 8, after % 8))

    @pl.when(me > 0)
    def _():
        to_before.start()

    @pl.when(me < 127)
    def _():
        to_after.start()

    def rp_hop(source, w, d, i, count=STEP, view=rows):
        n = 2 * source + w
        c = view(rp, 512 * source + 256 * w + STEP * i, count)
        return (
            remote(c, c, rpx.at[n], rp_in.at[n, i], next_x[w]), far_x[source][w],
            remote(c, c, rpy.at[n], rp_in.at[n, i], next_y[w]), far_y[w],
        )

    def panel_hop(source, w, kind, i, count=16):
        n = 2 * source + w
        c = rows(rp, 512 * source + 256 * w + 128 * kind + 16 * i, count)
        return (
            remote(c, c, pnx.at[n + 4 * kind], pn_in.at[n, i + 8 * kind], next_x[w]),
            b_far_x[source][w] if kind else a_far_x[source][w],
            remote(c, c, pny.at[n + 4 * kind], pn_in.at[n, i + 8 * kind], next_y[w]),
            b_far_y[source][w] if kind else a_far_y[source][w],
        )

    def pv_hop(source, w, d, i, src, count=STEP):
        n = 2 * source + w
        view = half if source else rows
        first = 512 * source + 256 * w + STEP * i
        return (
            remote(view(src, first, count), view(pv, first, count), pvz.at[n], pv_in.at[n, i], next_z[w]), far_z[w],
            remote(view(src, first, count), view(pv, first, count), pvc.at[n], pv_in.at[n, i], other), first_core,
        )

    def xr_hop(w, d, i, count=STEP):
        c = rows(xr, 256 * w + STEP * i, count)
        return (
            remote(c, c, xrz.at[w], xr_in.at[w, i], next_z[w]), far_z[w],
            remote(c, c, xrc.at[w], xr_in.at[w, i], other), first_core,
        )

    def pass_on(hop, received=True):
        one, p1, two, p2 = hop
        if received:
            one.wait_recv()

        @pl.when(p1)
        def _():
            one.start()

        @pl.when(p2)
        def _():
            two.start()

    def pivot_slot(t):
        for source in range(2):
            view = half if source else rows
            for w, d in ways():
                i = t - NSTEP * source - lag_xy[source][w]

                @pl.when(origin & (i >= 0) & (i < NSTEP))
                def _():
                    pass_on(rp_hop(source, w, d, i, STEP, view))
                    pass_on(pv_hop(source, w, d, i, rp), False)

                j = i - lag_z[w]

                @pl.when(~origin & (j >= 0) & (j < NSTEP))
                def _():
                    pass_on(pv_hop(source, w, d, j, pv))

    def panel_slot(t):
        for source in range(2):
            for w, _ in ways():
                for kind, lag in ((0, lag_a[source][w]), (1, lag_yx[source][w])):
                    i = t - 8 * source - lag

                    @pl.when(~origin & (i >= 0) & (i < 8))
                    def _():
                        pass_on(panel_hop(source, w, kind, i))

        for w, d in ways():
            i = t - 14 - lag_z[w]

            @pl.when((i >= 0) & (i < NSTEP))
            def _():
                pass_on(xr_hop(w, d, i))

    def gather_hook(e, b):
        @pl.when(lax.rem(b, 6) == 0)
        def _():
            pivot_slot(7 * e + lax.div(b, 6))

        @pl.when(lax.rem(b, 12) == 3)
        def _():
            panel_slot(4 * e + lax.div(b, 12))

    def contract_hook(e, a4):
        @pl.when(lax.rem(a4, 2) == 0)
        def _():
            pivot_slot(7 * e + 4 + lax.div(a4, 2))

        @pl.when((a4 == 1) | (a4 == 3))
        def _():
            panel_slot(4 * e + 2 + lax.div(a4, 2))

    @pl.when(me > 0)
    def _():
        to_before.wait_send()
        to_after.wait_recv()

    @pl.when(me < 127)
    def _():
        to_after.wait_send()
        to_before.wait_recv()

    applied[...] = jnp.zeros_like(applied)
    loads[0].wait()
    sub = lax.broadcasted_iota(jnp.int32, (256, 128), 0)

    def chunk(e, _):
        es = pl.ds(pl.multiple_of(e * 128, 128), 128)

        def gather(b, _):
            gather_hook(e, b)
            got[b] = pick(ext, dofs[b, :, es], 18)
            return 0

        lax.fori_loop(0, 24, gather, 0)

        def contract(a4, _):
            contract_hook(e, a4)
            total = [jnp.zeros((64, 128), F32) for _ in range(4)]
            for b in range(24):
                g = got[b]
                for q in range(4):
                    total[q] = total[q] + mass[a4 * 4 + q, pl.ds(b, 1), es] * g
            for q in range(4):
                a = a4 * 4 + q
                index = dofs[a, :, es]
                high = jnp.broadcast_to(index >> 8, (64, 128))
                low = jnp.broadcast_to(index & 255, (256, 128))
                big = total[q].astype(BF16).astype(F32)
                small = total[q] - big
                ps = pl.ds(pl.multiple_of(a * 128, 128), 128)
                for c in range(8):
                    here = high == c
                    wide[64 * c : 64 * c + 64, ps] = jnp.where(here, big, 0.0).astype(BF16)
                    wide[512 + 64 * c : 576 + 64 * c, ps] = jnp.where(here, small, 0.0).astype(BF16)
                hot[:, ps] = jnp.where(sub == low, 1.0, 0.0).astype(BF16)
            return 0

        lax.fori_loop(0, 6, contract, 0)
        out = lax.dot_general(wide[...], hot[...], NT, preferred_element_type=F32)
        for c in range(8):
            applied[:, 256 * c : 256 * c + 256] += out[64 * c : 64 * c + 64] + out[512 + 64 * c : 576 + 64 * c]
        return 0

    lax.fori_loop(0, 4, chunk, 0)

    lines = [device(x, y, z, 1 - k)]
    lines += [device(x + s, y, z, k) for s in (1, 2, 3)]
    lines += [device(x, y + s, z, k) for s in (1, 2, 3)]
    lines += [device(x, y, z + s, k) for s in (1, 2, 3)]

    def sum_copies(phase, stage):
        if stage == 0:
            return [remote(acc.at[phase, 0], core_slot.at[phase], send.at[phase, 0], recv.at[phase, 0], lines[0])]
        return [
            remote(acc.at[phase, stage], slots.at[phase, n - 1], send.at[phase, n], recv.at[phase, n], lines[n])
            for n in range(3 * stage - 2, 3 * stage + 1)
        ]

    def start_sum(phase, stage):
        for c in sum_copies(phase, stage):
            c.start()

    def finish_sum(phase, stage):
        for c in sum_copies(phase, stage):
            c.wait()
        value = acc[phase, stage]
        if stage == 0:
            acc[phase, 1] = value + core_slot[phase]
            return
        coordinate = (x, y, z)[stage - 1]
        parts = [value] + [slots[phase, 3 * stage - 4 + s] for s in (1, 2, 3)]
        ordered = []
        for q in range(4):
            away = (coordinate - q + 4) % 4
            part = parts[3]
            for s in (2, 1, 0):
                part = jnp.where(away == s, parts[s], part)
            ordered.append(part)
        acc[phase, stage + 1] = (ordered[0] + ordered[1]) + (ordered[2] + ordered[3])

    row, col = lax.axis_index("row"), lax.axis_index("col")
    shift = (bounds[0] + bounds[1]).astype(F32) / 510.0
    ri = lax.broadcasted_iota(jnp.int32, (512, 512), 0)
    ci = lax.broadcasted_iota(jnp.int32, (512, 512), 1)

    def pivot(ref, r, c, shifted):
        for where, src in ((col == 0, rp), (col > 0, pv)):
            @pl.when(where)
            def _():
                block = src[r : r + 512, c : c + 512]
                if shifted:
                    block = block - jnp.where(ri == ci, shift * diag[:, c : c + 512], 0.0)
                ref[...] = block

    loads[1].wait()
    acc[0, 0] = dot(applied[...], basis[...], NT)
    start_sum(0, 0)
    loads[2].wait()
    pivot(a11, 0, 0, True)

    @pl.when((row == 0) & (col == 0))
    def _():
        out[:, 0:512] = a11[...]

    def first_slots(b, q):
        if q % 2 == 0:
            pivot_slot(28 + 2 * b + q // 2)
        else:
            panel_slot(16 + 2 * b + q // 2)

    def last_slots(b, q):
        if q % 2 == 1:
            panel_slot(24 + 2 * b + q // 2)

    def advance(phase, b):
        for stage in range(4):
            @pl.when(b == stage)
            def _():
                finish_sum(phase, stage)
                if stage < 3:
                    start_sum(phase, stage + 1)

    invert_in_place(a11, first_slots, functools.partial(advance, 0))

    pt = acc[0, 4] / TOTAL
    proj[...] = pt
    corrected = applied[...] - dot(pt, basis[...])
    applied[...] = corrected
    acc[1, 0] = jnp.concatenate([dot(corrected, corrected, NT), jnp.zeros((64, 64), F32)], axis=1)
    start_sum(1, 0)

    pivot(a12, 0, 512, False)
    pivot(a22, 512, 512, True)
    w = dot(a11[...], a12[...])
    s22 = a22[...] - dot(a12[...], w, TN)
    a12[...] = w
    a22[...] = s22

    @pl.when((row == 1) & (col == 0))
    def _():
        out[:, 0:512] = jnp.transpose(w)
        out[:, 512:1024] = s22

    @pl.when((row == 0) & (col == 0))
    def _():
        out[:, 512:1024] = w

    invert_in_place(a22, last_slots, functools.partial(advance, 1))

    @pl.when(row >= 2)
    def _():
        x1, x2 = split(xr[:, 0:512]), xr[:, 512:1024]
        i2, ws = split(a22[...]), split(a12[...])
        l1 = dot3(x1, split(a11[...]))
        l2 = dot3(split(x2 - dot3(x1, ws)), i2)

        @pl.when(col == 0)
        def _():
            out[:, 0:512] = l1
            out[:, 512:1024] = l2

        @pl.when(col > 0)
        def _():
            l2s = split(l2)
            t1 = split(l1 - dot3(l2s, ws, NT))
            j = lax.broadcasted_iota(jnp.int32, (512, 1024), 1)
            i = lax.broadcasted_iota(jnp.int32, (512, 1024), 0)
            mine = diag[:, pl.ds(pl.multiple_of(col * 1024, 1024), 1024)]
            tile = out[...] - jnp.where(j + col * 1024 == i + row * 512, shift * mine, 0.0)
            out[...] = tile - dot3(t1, split(rp[0:512, :])) - dot3(l2s, split(rp[512:1024, :]))

    @pl.when((row == 0) & (col > 0))
    def _():
        out[...] = dot3(split(a11[...]), split(rp[0:512, :]))

    @pl.when((row == 1) & (col > 0))
    def _():
        out[...] = dot3(split(a22[...]), split(rp[512:1024, :] - dot3(split(a12[...]), split(rp[0:512, :]), TN)))

    gram = acc[1, 4] / TOTAL
    lane8 = lax.broadcasted_iota(jnp.int32, (8, 128), 1)
    row8 = lax.broadcasted_iota(jnp.int32, (8, 128), 0)
    v = [gram[8 * i : 8 * i + 8] + jnp.where(lane8 == row8 + 64 + 8 * i, 1.0, 0.0) for i in range(8)]
    for kb in range(8):
        k0 = 8 * kb
        w = v[kb]
        first = [lanes(w, k0 + j) for j in range(8)]
        cols = inverse8(first, row8)
        r = tree([cols[m] * subs(w, m) for m in range(8)])
        rs = [subs(r, m) for m in range(8)]
        for i in range(kb + 1, 8):
            o = v[i]
            v[i] = o - tree([lanes(o, k0 + m) * rs[m] for m in range(8)])
        c = list(first)
        scale = jnp.zeros((8, 128), F32)
        for j in range(8):
            p = subs(c[j], j)
            f = jnp.where(row8 > j, c[j] / p, 0.0)
            w = w - f * subs(w, j)
            for m in range(j + 1, 8):
                c[m] = c[m] - f * subs(c[m], j)
            scale = jnp.where(row8 == j, p, scale)
        v[kb] = w / jnp.sqrt(scale)
    full = jnp.concatenate(v, 0)
    upper, inverse = full[:, 0:64], full[:, 64:128]
    ri = lax.broadcasted_iota(jnp.int32, (64, 64), 0)
    ci = lax.broadcasted_iota(jnp.int32, (64, 64), 1)
    chol[...] = jnp.transpose(jnp.where(ri <= ci, upper, 0.0))
    new[...] = dot(inverse, applied[...])

    def drain(hop):
        one, p1, two, p2 = hop

        @pl.when(p1)
        def _():
            one.wait_send()

        @pl.when(p2)
        def _():
            two.wait_send()

    for w, d in ways():
        drain(xr_hop(w, d, 0, 256))

        @pl.when(origin)
        def _():
            drain(rp_hop(0, w, d, 0, 256))
            drain(rp_hop(1, w, d, 0, 256, half))

        @pl.when(~origin)
        def _():
            for source in range(2):
                for kind in range(2):
                    drain(panel_hop(source, w, kind, 0, 128))

        for source in range(2):
            drain(pv_hop(source, w, d, 0, pv, 256))


def step(bounds, diag, vectors, dofs, faces, front, mass, basis):
    dma = pltpu.SemaphoreType.DMA
    return pl.pallas_call(
        step_kernel,
        out_shape=(
            jax.ShapeDtypeStruct((512, 1024), F32),
            jax.ShapeDtypeStruct((64, 2048), F32),
            jax.ShapeDtypeStruct((64, 128), F32),
            jax.ShapeDtypeStruct((64, 64), F32),
        ),
        in_specs=[pl.BlockSpec(memory_space=pltpu.SMEM), VM, VM, VM, VM, ANY, ANY, ANY],
        out_specs=(VM, VM, VM, VM),
        scratch_shapes=[
            pltpu.VMEM((24, 1, 512), jnp.int32),
            pltpu.VMEM((512, 1024), F32),
            pltpu.VMEM((1024, 1024), F32),
            pltpu.VMEM((1024, 1024), F32),
            pltpu.VMEM((64, 2048), F32),
            pltpu.VMEM((64, 2304), F32),
            pltpu.VMEM((2, 64, 128), F32),
            pltpu.VMEM((24, 64, 128), F32),
            pltpu.VMEM((1024, 3072), BF16),
            pltpu.VMEM((256, 3072), BF16),
            pltpu.VMEM((24, 24, 512), F32),
            pltpu.VMEM((128, 2048), F32),
            pltpu.VMEM((512, 512), F32),
            pltpu.VMEM((512, 512), F32),
            pltpu.VMEM((512, 512), F32),
            pltpu.VMEM((2, 5, 64, 128), F32),
            pltpu.VMEM((2, 9, 64, 128), F32),
            pltpu.VMEM((2, 64, 128), F32),
            dma((4, NSTEP)), dma((4, 16)), dma((8,)), dma((8,)), dma((4, NSTEP)), dma((2, NSTEP)),
            dma((4,)), dma((4,)), dma((4,)), dma((4,)), dma((2,)), dma((2,)),
            dma((2,)), dma((2,)), dma((3,)), dma((2, 10)), dma((2, 10)),
        ],
        compiler_params=pltpu.CompilerParams(collective_id=1, has_side_effects=True, vmem_limit_bytes=60 << 20),
    )(bounds, diag, vectors, dofs, faces, front, mass, basis)


def shards(front, mass_diag, shift_bounds, vectors, basis, element_dofs, face_dofs, mass_blocks):
    factor, new_block, projections, cholesky_factor = step(
        shift_bounds, mass_diag.reshape(1, -1), vectors,
        element_dofs, face_dofs, front, mass_blocks, basis,
    )
    return factor, new_block, projections.T, cholesky_factor


def solution(mesh):
    placed = (
        P("row", "col"),
        P(),
        P(),
        P(None, ("row", "col")),
        P(None, ("row", "col")),
        P(None, ("row", "col")),
        P(("row", "col"), None),
        P(None, None, ("row", "col")),
    )
    return jax.shard_map(
        shards,
        mesh=mesh,
        in_specs=placed,
        out_specs=(P("row", "col"), P(None, ("row", "col")), P(), P()),
        check_vma=False,
    )
```
